256 devices in a mesh: seq: 32 (over y_lo, z, core), head: 8 (over y_hi, x).
Axes of the slice: x: 4, y: 4 (y_hi: 2, y_lo: 2; y = y_hi * 2 + y_lo), z: 8, core: 2. Of those that a mesh axis runs over, the one named last changes fastest.
Arguments:
- inputs: bfloat16 [16384, 5376], P('seq'), may hold values from -6 to 6
- queries: bfloat16 [16384, 4096], P('seq', 'head'), may hold values from -6 to 6
- key_matrix: bfloat16 [5376, 2048], P('seq', 'head'), may hold values from -0.078125 to 0.078125
- value_matrix: bfloat16 [5376, 2048], P('seq', 'head'), may hold values from -0.078125 to 0.078125
- readout: bfloat16 [4096, 512], P('head'), may hold values from -6 to 6
- token_mask: int32 [16384], P('seq'), may hold values 0 or 1
- targets: int32 [16384], P('seq'), may hold values from 0 to 511
Outputs:
- query_grad: float32 [16384, 4096], P('seq', 'head')
- input_grad: float32 [16384, 5376], P('seq', 'head')
The draws below stay inside these ranges and needn't reach their ends.
All inputs are finite; a program needn't handle non-finite values. No bound on the sum of `token_mask` on one device may be relied on, other than what follows from the above.
Results may differ from the reference program's by a relative error of at most 0.028.
Values may be sent and summed in bfloat16 or wider, within the bound.
No kernel may reach another device: no remote copies, remote signals or barrier semaphores. Data moves between devices by JAX's collectives and lax.ppermute only.
A program may use at most 128 MiB of HBM per device.

```python
import jax
import jax.numpy as jnp
from jax import lax

MODEL_WIDTH = 5376
QUERY_HEADS = 32
KEY_VALUE_HEADS = 16
HEAD_SIZE = 128
WINDOW_KEYS = 1024
LOCAL_TOKENS = 512
CAND = 512
SEQUENCE_TOKENS = 16384
N_HEAD = 8


def plant(array, rng, low, high):
    longest = array.shape.index(max(array.shape))
    spots = []
    for shift in (0, 1):
        where = [jax.random.randint(jax.random.fold_in(rng, axis), (), 0, length) for axis, length in enumerate(array.shape)]
        where[longest] = (where[longest] + shift) % array.shape[longest]
        spots.append(tuple(where))
    return array.at[spots[0]].set(low).at[spots[1]].set(high)


def level_of(rng, extent, cuts, smallest, top_value):
    gain = 1.0
    for position, shards_of in cuts:
        heights = jax.random.uniform(jax.random.fold_in(jax.random.fold_in(rng, 6), position), (shards_of,), jnp.float32, smallest / len(cuts), top_value / len(cuts))
        gain = gain * jnp.repeat(jnp.exp(heights), extent[position] // shards_of).reshape((-1,) + (1,) * (len(extent) - 1 - position))
    return gain


def scatter_about(own_key, dims, scale, limit, cuts=(), kind=jnp.bfloat16):
    result = jax.random.normal(own_key, dims, jnp.float32) * scale
    if len(cuts) > 0:
        result = level_of(own_key, dims, cuts, -0.22, 0.18) * result
    return jnp.clip(result, min=-limit, max=limit).astype(kind)


def setup_inputs(seed: int = 0) -> dict:
    streams_of = jax.random.split(jax.random.key(seed), 8)
    return {
        "inputs": scatter_about(streams_of[0], (SEQUENCE_TOKENS, MODEL_WIDTH), 1.0, 6.0, ((0, 32),)),
        "queries": scatter_about(streams_of[1], (SEQUENCE_TOKENS, QUERY_HEADS * HEAD_SIZE), 1.0, 6.0, ((0, 32), (1, 8))),
        "key_matrix": scatter_about(streams_of[2], (MODEL_WIDTH, KEY_VALUE_HEADS * HEAD_SIZE), MODEL_WIDTH ** -0.5, 0.078125, ((0, 32), (1, 8))),
        "value_matrix": scatter_about(streams_of[3], (MODEL_WIDTH, KEY_VALUE_HEADS * HEAD_SIZE), MODEL_WIDTH ** -0.5, 0.078125, ((0, 32), (1, 8))),
        "readout": scatter_about(streams_of[4], (QUERY_HEADS * HEAD_SIZE, CAND), 1.0, 6.0, ((0, 8),)),
        "token_mask": plant((jax.random.randint(streams_of[5], (SEQUENCE_TOKENS,), 0, 5) < 1).astype(jnp.int32), jax.random.fold_in(streams_of[5], 1), 0, 1),
        "targets": plant(jax.random.randint(streams_of[6], (SEQUENCE_TOKENS,), 0, CAND), jax.random.fold_in(streams_of[6], 1), 0, CAND - 1).astype(jnp.int32),
    }


norm_eps = 1e-06
softcap = 30.0
score_scale = 168.0 ** (-0.5)

def normalized_rows(value_rows):
    inverse = lax.rsqrt(lax.optimization_barrier(jnp.mean(value_rows * value_rows, axis=-1, keepdims=True)) + norm_eps)
    return (value_rows * inverse, inverse)

def unit_norm_backward(unit, inverse, upstream):
    return inverse * (upstream - unit * lax.optimization_barrier(jnp.mean(unit * upstream, axis=-1, keepdims=True)))

def reference(inputs, queries, key_matrix, value_matrix, readout, token_mask, targets):
    query_groups = QUERY_HEADS // KEY_VALUE_HEADS
    span = WINDOW_KEYS + LOCAL_TOKENS
    blocks = SEQUENCE_TOKENS // LOCAL_TOKENS
    key_unscaled = jnp.dot(inputs, key_matrix, preferred_element_type=jnp.float32).reshape(SEQUENCE_TOKENS, KEY_VALUE_HEADS, HEAD_SIZE)
    value_rows = jnp.dot(inputs, value_matrix, preferred_element_type=jnp.float32).astype(jnp.bfloat16).reshape(SEQUENCE_TOKENS, KEY_VALUE_HEADS, HEAD_SIZE)
    key_unit_rows, key_inverse_norm = normalized_rows(key_unscaled)
    key_normalized_rows = key_unit_rows.astype(jnp.bfloat16)
    query_unit_rows, query_inverse_norm = normalized_rows(queries.astype(jnp.float32).reshape(SEQUENCE_TOKENS, KEY_VALUE_HEADS, query_groups, HEAD_SIZE))
    query_hat = query_unit_rows.astype(jnp.bfloat16)
    padded_keys = jnp.concatenate([jnp.zeros((WINDOW_KEYS, KEY_VALUE_HEADS, HEAD_SIZE), jnp.bfloat16), key_normalized_rows], axis=0)
    padded_values = jnp.concatenate([jnp.zeros((WINDOW_KEYS, KEY_VALUE_HEADS, HEAD_SIZE), jnp.bfloat16), value_rows], axis=0)
    readout_f = readout.astype(jnp.float32)

    def one_block(carry, index):
        key_running_sum, value_running_sum = carry
        start = (index * LOCAL_TOKENS).astype(jnp.int32)
        q_block = lax.dynamic_slice_in_dim(query_hat, start, LOCAL_TOKENS, 0).astype(jnp.float32)
        q_unit = lax.dynamic_slice_in_dim(query_unit_rows, start, LOCAL_TOKENS, 0)
        q_inverse = lax.dynamic_slice_in_dim(query_inverse_norm, start, LOCAL_TOKENS, 0)
        k_block = lax.dynamic_slice_in_dim(padded_keys, start, span, 0).astype(jnp.float32)
        v_block = lax.dynamic_slice_in_dim(padded_values, start, span, 0).astype(jnp.float32)
        chosen = lax.dynamic_slice_in_dim(token_mask, start, LOCAL_TOKENS, 0).astype(jnp.float32)[:, None]
        wanted = lax.dynamic_slice_in_dim(targets, start, LOCAL_TOKENS, 0)
        query_pos = start + jnp.arange(LOCAL_TOKENS, dtype=jnp.int32)
        key_pos = start - WINDOW_KEYS + jnp.arange(span, dtype=jnp.int32)
        distance = query_pos[:, None] - key_pos[None, :]
        visible = (distance >= 0) & (distance < WINDOW_KEYS) & (key_pos[None, :] >= 0)
        scores = jnp.einsum('qkgd,jkd->kgqj', q_block, k_block) * score_scale
        raised = jnp.where(visible, jnp.exp(scores), 0.0)
        attn = (raised / lax.optimization_barrier(jnp.sum(raised, axis=-1, keepdims=True))).astype(jnp.bfloat16)
        attn_f = attn.astype(jnp.float32)
        attended = jnp.einsum('kgqj,jkd->qkgd', attn_f, v_block).astype(jnp.bfloat16)
        flat = attended.reshape(LOCAL_TOKENS, QUERY_HEADS * HEAD_SIZE)
        logits = jnp.dot(flat, readout, preferred_element_type=jnp.float32)
        capped = softcap * jnp.tanh(logits / softcap)
        expo = jnp.exp(capped)
        probs = expo / lax.optimization_barrier(jnp.sum(expo, axis=-1, keepdims=True))
        onehot = (wanted[:, None] == jnp.arange(CAND, dtype=jnp.int32)[None, :]).astype(jnp.float32)
        dlogits = (chosen * (probs - onehot) * (1.0 - (capped / softcap) ** 2)).astype(jnp.bfloat16)
        attended_grad = jnp.dot(dlogits.astype(jnp.float32), readout_f.T).astype(jnp.bfloat16)
        attention_grad = attended_grad.astype(jnp.float32).reshape(LOCAL_TOKENS, KEY_VALUE_HEADS, query_groups, HEAD_SIZE)
        d_weights = jnp.einsum('qkgd,jkd->kgqj', attention_grad, v_block)
        d_scores = (attn_f * (d_weights - lax.optimization_barrier(jnp.sum(attn_f * d_weights, axis=-1, keepdims=True)))).astype(jnp.bfloat16).astype(jnp.float32)
        d_query_hat = jnp.einsum('kgqj,jkd->qkgd', d_scores, k_block) * score_scale
        d_key_hat = jnp.einsum('kgqj,qkgd->jkd', d_scores, q_block) * score_scale
        d_value = jnp.einsum('kgqj,qkgd->jkd', attn_f, attention_grad)
        q_grad = unit_norm_backward(q_unit, q_inverse, d_query_hat).reshape(LOCAL_TOKENS, QUERY_HEADS * HEAD_SIZE)
        key_running_sum = lax.dynamic_update_slice_in_dim(key_running_sum, lax.dynamic_slice_in_dim(key_running_sum, start, span, 0) + d_key_hat, start, 0)
        value_running_sum = lax.dynamic_update_slice_in_dim(value_running_sum, lax.dynamic_slice_in_dim(value_running_sum, start, span, 0) + d_value, start, 0)
        return ((key_running_sum, value_running_sum), q_grad)
    empty_running_sum = jnp.zeros((WINDOW_KEYS + SEQUENCE_TOKENS, KEY_VALUE_HEADS, HEAD_SIZE), jnp.float32)
    (key_running_sum, value_running_sum), q_grads = lax.scan(one_block, (empty_running_sum, empty_running_sum), jnp.arange(blocks, dtype=jnp.int32))
    query_grad = q_grads.reshape(SEQUENCE_TOKENS, QUERY_HEADS * HEAD_SIZE)
    key_weight_gradient = unit_norm_backward(key_unit_rows, key_inverse_norm, key_running_sum[WINDOW_KEYS:]).astype(jnp.bfloat16).reshape(SEQUENCE_TOKENS, KEY_VALUE_HEADS * HEAD_SIZE)
    value_weight_gradient = value_running_sum[WINDOW_KEYS:].astype(jnp.bfloat16).reshape(SEQUENCE_TOKENS, KEY_VALUE_HEADS * HEAD_SIZE)
    group_columns = KEY_VALUE_HEADS * HEAD_SIZE // N_HEAD
    input_grad = jnp.zeros((SEQUENCE_TOKENS, MODEL_WIDTH), jnp.float32)
    for group in range(N_HEAD):
        low = group * group_columns
        grads = jnp.concatenate([key_weight_gradient[:, low:low + group_columns], value_weight_gradient[:, low:low + group_columns]], axis=1)
        weights = jnp.concatenate([key_matrix[:, low:low + group_columns], value_matrix[:, low:low + group_columns]], axis=1)
        term = jnp.dot(grads, weights.T, preferred_element_type=jnp.float32).astype(jnp.bfloat16)
        input_grad = input_grad + term.astype(jnp.float32)
    return (query_grad, input_grad)
```

```python
import jax
import jax.numpy as jnp
from jax import lax
from jax.sharding import PartitionSpec as P

HEAD_SIZE = 128
WINDOW_KEYS = 1024

norm_eps = 1e-06
softcap = 30.0
score_scale = 168.0 ** (-0.5)

Y_LO, Z, CORES = 2, 8, 2
Y_HI, X = 2, 4


def seq_pairs(move):
    pairs = []
    for y in range(Y_LO):
        for z in range(Z):
            for c in range(CORES):
                ty, tz, tc = move(y, z, c)
                pairs.append(((y * Z + z) * CORES + c, (ty * Z + tz) * CORES + tc))
    return pairs


CORE_SWAP = seq_pairs(lambda y, z, c: (y, z, 1 - c))
Y_SWAP = seq_pairs(lambda y, z, c: (1 - y, z, c))
Z_UP = seq_pairs(lambda y, z, c: (y, (z + 1) % Z, c))
Z_DOWN = seq_pairs(lambda y, z, c: (y, (z - 1) % Z, c))


def head_pairs(flip, steps):
    return [
        (y * X + x, (y ^ flip) * X + (x + steps) % X) for y in range(Y_HI) for x in range(X)
    ]


X_UP, X_DOWN, Y_HI_SWAP = head_pairs(0, 1), head_pairs(0, -1), head_pairs(1, 0)


def weight_rows(own):
    rows, columns = own.shape
    heads, per_head = Y_HI * X, Y_LO * Z * CORES // (Y_HI * X)
    pairs = [
        ((per_head * h + r) * heads + g, (per_head * g + r) * heads + h)
        for h in range(heads)
        for r in range(per_head)
        for g in range(heads)
    ]
    moved = lax.ppermute(own, ("seq", "head"), pairs)
    return lax.all_gather(moved, "seq", axis=0, tiled=True).reshape(heads, -1, columns)


def head_product(weight, own):
    head = lax.axis_index("head")
    y, x = head // X, head % X

    def send(value, pairs):
        return lax.ppermute(value, "head", pairs)

    def term(value, flip, steps):
        block = lax.dynamic_index_in_dim(
            weight, (y ^ flip) * X + jnp.mod(x - steps, X), 0, keepdims=False
        )
        return lax.dot_general(
            block, value, (((1,), (1,)), ((), ())), preferred_element_type=jnp.float32
        )

    half = own.shape[0] // 2
    below, above, across = send(own, X_UP), send(own, X_DOWN), send(own, Y_HI_SWAP)
    far = jnp.concatenate([send(below[:half], X_UP), send(above[half:], X_DOWN)])
    across_below, across_above = send(across, X_UP), send(across, X_DOWN)
    across_far = send(far, Y_HI_SWAP)
    total = term(own, 0, 0)
    for value, flip, steps in (
        (below, 0, 1),
        (above, 0, -1),
        (across, 1, 0),
        (far, 0, 2),
        (across_below, 1, 1),
        (across_above, 1, -1),
        (across_far, 1, 2),
    ):
        total = total + term(value, flip, steps)
    return total


def along(value, steps):
    count = lax.axis_size("seq")
    first, last = max(0, -steps), min(count, count - steps)
    return lax.ppermute(value, "seq", [(i, i + steps) for i in range(first, last)])


def gathered_weights(own):
    rows, columns = own.shape
    seq = lax.axis_index("seq")
    y, z, core = seq // (Z * CORES), (seq // CORES) % Z, seq % CORES
    other = lax.ppermute(own, "seq", Y_SWAP)
    low = jnp.where(y == 0, own, other)
    high = jnp.where(y == 0, other, own)
    pair = jnp.stack([low, high])
    full = jnp.zeros((Y_LO, Z, CORES, rows, columns), own.dtype)

    def put(full, block, from_z):
        swapped = lax.ppermute(block, "seq", CORE_SWAP)
        at = jnp.mod(z + from_z, Z)
        for piece, c in ((block, core), (swapped, 1 - core)):
            full = lax.dynamic_update_slice(full, piece[:, None, None], (0, at, c, 0, 0))
        return full

    up = down = pair
    full = put(full, pair, 0)
    for k in range(1, Z // 2):
        up = lax.ppermute(up, "seq", Z_UP)
        down = lax.ppermute(down, "seq", Z_DOWN)
        full = put(full, up, -k)
        full = put(full, down, k)
    last = jnp.stack(
        [lax.ppermute(up[0], "seq", Z_UP), lax.ppermute(down[1], "seq", Z_DOWN)]
    )
    full = put(full, last, Z // 2)
    return full.reshape(Y_LO * Z * CORES * rows, columns)


def normalized_rows(value_rows):
    inverse = lax.rsqrt(jnp.mean(value_rows * value_rows, axis=-1, keepdims=True) + norm_eps)
    return (value_rows * inverse, inverse)


def unit_norm_backward(unit, inverse, upstream):
    return inverse * (upstream - unit * jnp.mean(unit * upstream, axis=-1, keepdims=True))


def shards(inputs, queries, key_matrix, value_matrix, readout, token_mask, targets):
    tokens = inputs.shape[0]
    kv_width = key_matrix.shape[1]
    kv_heads = kv_width // HEAD_SIZE
    q_heads = queries.shape[1] // HEAD_SIZE
    query_groups = q_heads // kv_heads
    heads = lax.axis_size("head")
    seq = lax.axis_index("seq")
    core = seq % CORES
    span = 3 * tokens
    own_weight = jnp.concatenate([key_matrix, value_matrix], axis=1)
    full_weight = gathered_weights(own_weight)
    own_weight, _ = lax.optimization_barrier((own_weight, full_weight[:8, :128]))
    rows_weight = weight_rows(own_weight)
    projected = jnp.dot(inputs, full_weight, preferred_element_type=jnp.float32)
    key_unscaled = projected[:, :kv_width].reshape(tokens, kv_heads, HEAD_SIZE)
    value_rows = projected[:, kv_width:].astype(jnp.bfloat16).reshape(tokens, kv_heads, HEAD_SIZE)
    key_unit_rows, key_inverse_norm = normalized_rows(key_unscaled)
    key_normalized_rows = key_unit_rows.astype(jnp.bfloat16)
    query_unit_rows, query_inverse_norm = normalized_rows(
        queries.astype(jnp.float32).reshape(tokens, kv_heads, query_groups, HEAD_SIZE)
    )
    query_hat = query_unit_rows.astype(jnp.bfloat16)
    paired = jnp.concatenate([key_normalized_rows, value_rows], axis=-1)
    second = along(paired, 2)
    first = lax.ppermute(jnp.where(core == 0, paired, second), "seq", CORE_SWAP)
    window_kv = jnp.concatenate([second, first, paired], axis=0)
    key_block = window_kv[..., :HEAD_SIZE]
    value_block = window_kv[..., HEAD_SIZE:]
    start = seq * tokens
    query_pos = start + jnp.arange(tokens, dtype=jnp.int32)
    key_pos = start - 2 * tokens + jnp.arange(span, dtype=jnp.int32)
    distance = query_pos[:, None] - key_pos[None, :]
    visible = (distance >= 0) & (distance < WINDOW_KEYS) & (key_pos[None, :] >= 0)
    scores = (
        jnp.einsum("qkgd,jkd->kgqj", query_hat, key_block, preferred_element_type=jnp.float32)
        * score_scale
    )
    raised = jnp.where(visible, jnp.exp(scores), 0.0)
    attn = (raised / jnp.sum(raised, axis=-1, keepdims=True)).astype(jnp.bfloat16)
    attended = jnp.einsum(
        "kgqj,jkd->qkgd", attn, value_block, preferred_element_type=jnp.float32
    ).astype(jnp.bfloat16)
    flat = attended.reshape(tokens, q_heads * HEAD_SIZE)
    partial_value = jnp.dot(flat, readout, preferred_element_type=jnp.float32)

    share = tokens // heads
    terms = lax.all_to_all(partial_value.astype(jnp.bfloat16), "head", 0, 0, tiled=True)
    logits = jnp.sum(terms.astype(jnp.float32).reshape(heads, share, -1), axis=0)
    mine = lax.axis_index("head") * share
    wanted = lax.dynamic_slice_in_dim(targets, mine, share, 0)
    chosen = lax.dynamic_slice_in_dim(token_mask, mine, share, 0).astype(jnp.float32)[:, None]
    capped = softcap * jnp.tanh(logits / softcap)
    expo = jnp.exp(capped)
    probs = expo / jnp.sum(expo, axis=-1, keepdims=True)
    onehot = (wanted[:, None] == jnp.arange(logits.shape[1], dtype=jnp.int32)[None, :]).astype(
        jnp.float32
    )
    dlogits = (chosen * (probs - onehot) * (1.0 - (capped / softcap) ** 2)).astype(jnp.bfloat16)
    dlogits = lax.all_to_all(
        jnp.broadcast_to(dlogits[None], (heads,) + dlogits.shape), "head", 0, 0, tiled=True
    ).reshape(tokens, -1)

    attended_grad = lax.dot_general(
        dlogits, readout, (((1,), (1,)), ((), ())), preferred_element_type=jnp.float32
    )
    attended_grad = attended_grad.astype(jnp.bfloat16).reshape(
        tokens, kv_heads, query_groups, HEAD_SIZE
    )
    d_weights = jnp.einsum(
        "qkgd,jkd->kgqj", attended_grad, value_block, preferred_element_type=jnp.float32
    )
    attn_f = attn.astype(jnp.float32)
    d_scores = (attn_f * (d_weights - jnp.sum(attn_f * d_weights, axis=-1, keepdims=True))).astype(
        jnp.bfloat16
    )
    d_query_hat = (
        jnp.einsum("kgqj,jkd->qkgd", d_scores, key_block, preferred_element_type=jnp.float32)
        * score_scale
    )
    d_key_hat = (
        jnp.einsum("kgqj,qkgd->jkd", d_scores, query_hat, preferred_element_type=jnp.float32)
        * score_scale
    )
    d_value = jnp.einsum("kgqj,qkgd->jkd", attn, attended_grad, preferred_element_type=jnp.float32)
    query_grad = unit_norm_backward(query_unit_rows, query_inverse_norm, d_query_hat).reshape(
        tokens, q_heads * HEAD_SIZE
    )
    pieces = jnp.concatenate([d_key_hat, d_value], axis=-1)
    to_second, to_first, total = (
        pieces[i * tokens : (i + 1) * tokens] for i in range(3)
    )
    crossed = lax.ppermute(to_first.astype(jnp.bfloat16), "seq", CORE_SWAP).astype(jnp.float32)
    outgoing = to_second + jnp.where(core == 1, crossed, 0.0)
    arrived = along(outgoing.astype(jnp.bfloat16), -2).astype(jnp.float32)
    total = total + arrived + jnp.where(core == 0, crossed, 0.0)
    key_weight_gradient = (
        unit_norm_backward(key_unit_rows, key_inverse_norm, total[..., :HEAD_SIZE])
        .astype(jnp.bfloat16)
        .reshape(tokens, kv_width)
    )
    value_weight_gradient = total[..., HEAD_SIZE:].astype(jnp.bfloat16).reshape(tokens, kv_width)
    both_grad = jnp.concatenate([key_weight_gradient, value_weight_gradient], axis=1)
    input_grad = head_product(rows_weight, both_grad).T
    return (query_grad, input_grad)


def solution(mesh):
    in_specs = (
        P("seq", None),
        P("seq", "head"),
        P("seq", "head"),
        P("seq", "head"),
        P("head", None),
        P("seq"),
        P("seq"),
    )
    out_specs = (P("seq", "head"), P("seq", "head"))
    return jax.shard_map(shards, mesh=mesh, in_specs=in_specs, out_specs=out_specs, check_vma=False)
```

```python
import jax
import jax.numpy as jnp
from jax import lax
from jax.experimental import pallas as pl
from jax.experimental.pallas import tpu as pltpu
from jax.sharding import PartitionSpec as P

HEAD_SIZE = 128
WINDOW_KEYS = 1024

norm_eps = 1e-06
softcap = 30.0
score_scale = 168.0 ** (-0.5)
LOG2_E = 1.4426950408889634

Y_LO, Z, CORES = 2, 8, 2
Y_HI, X = 2, 4


def seq_pairs(move):
    pairs = []
    for y in range(Y_LO):
        for z in range(Z):
            for c in range(CORES):
                ty, tz, tc = move(y, z, c)
                pairs.append(((y * Z + z) * CORES + c, (ty * Z + tz) * CORES + tc))
    return pairs


CORE_SWAP = seq_pairs(lambda y, z, c: (y, z, 1 - c))
Y_SWAP = seq_pairs(lambda y, z, c: (1 - y, z, c))
Z_UP = seq_pairs(lambda y, z, c: (y, (z + 1) % Z, c))
Z_DOWN = seq_pairs(lambda y, z, c: (y, (z - 1) % Z, c))


def head_pairs(flip, steps):
    return [
        (y * X + x, (y ^ flip) * X + (x + steps) % X) for y in range(Y_HI) for x in range(X)
    ]


X_UP, X_DOWN, Y_HI_SWAP = head_pairs(0, 1), head_pairs(0, -1), head_pairs(1, 0)


def weight_rows(own):
    rows, columns = own.shape
    heads, per_head = Y_HI * X, Y_LO * Z * CORES // (Y_HI * X)
    pairs = [
        ((per_head * h + r) * heads + g, (per_head * g + r) * heads + h)
        for h in range(heads)
        for r in range(per_head)
        for g in range(heads)
    ]
    moved = lax.ppermute(own, ("seq", "head"), pairs)
    return lax.all_gather(moved, "seq", axis=0, tiled=True).reshape(heads, -1, columns)


def head_product(weight, own):
    head = lax.axis_index("head")
    y, x = head // X, head % X

    def send(value, pairs):
        return lax.ppermute(value, "head", pairs)

    def term(value, flip, steps):
        block = lax.dynamic_index_in_dim(
            weight, (y ^ flip) * X + jnp.mod(x - steps, X), 0, keepdims=False
        )
        return lax.dot_general(
            block, value, (((1,), (1,)), ((), ())), preferred_element_type=jnp.float32
        )

    half = own.shape[0] // 2
    below, above, across = send(own, X_UP), send(own, X_DOWN), send(own, Y_HI_SWAP)
    far = jnp.concatenate([send(below[:half], X_UP), send(above[half:], X_DOWN)])
    across_below, across_above = send(across, X_UP), send(across, X_DOWN)
    across_far = send(far, Y_HI_SWAP)
    total = term(own, 0, 0)
    for value, flip, steps in (
        (below, 0, 1),
        (above, 0, -1),
        (across, 1, 0),
        (far, 0, 2),
        (across_below, 1, 1),
        (across_above, 1, -1),
        (across_far, 1, 2),
    ):
        total = total + term(value, flip, steps)
    return total


def along(value, steps):
    count = lax.axis_size("seq")
    first, last = max(0, -steps), min(count, count - steps)
    return lax.ppermute(value, "seq", [(i, i + steps) for i in range(first, last)])


def gathered_weights(own):
    rows, columns = own.shape
    seq = lax.axis_index("seq")
    y, z, core = seq // (Z * CORES), (seq // CORES) % Z, seq % CORES
    other = lax.ppermute(own, "seq", Y_SWAP)
    low = jnp.where(y == 0, own, other)
    high = jnp.where(y == 0, other, own)
    pair = jnp.stack([low, high])
    full = jnp.zeros((Y_LO, Z, CORES, rows, columns), own.dtype)

    def put(full, blocks):
        offsets = list(blocks)
        swapped = lax.ppermute(jnp.concatenate(list(blocks.values())), "seq", CORE_SWAP)
        for n, offset in enumerate(offsets):
            at = jnp.mod(z + offset, Z)
            for piece, c in ((blocks[offset], core), (swapped[2 * n : 2 * n + 2], 1 - core)):
                full = lax.dynamic_update_slice(full, piece[:, None, None], (0, at, c, 0, 0))
        return full

    up = down = pair
    full = put(full, {0: pair})
    for k in range(1, Z // 2):
        up = lax.ppermute(up, "seq", Z_UP)
        down = lax.ppermute(down, "seq", Z_DOWN)
        full = put(full, {-k: up, k: down})
    last = jnp.stack(
        [lax.ppermute(up[0], "seq", Z_UP), lax.ppermute(down[1], "seq", Z_DOWN)]
    )
    full = put(full, {Z // 2: last})
    return full.reshape(Y_LO * Z * CORES * rows, columns)


TILE = 128


def dot(a, b, contract):
    return lax.dot_general(a, b, ((contract[:1], contract[1:]), ((), ())), preferred_element_type=jnp.float32)


def unit_of(rows):
    rows = rows.astype(jnp.float32)
    inverse = lax.rsqrt(jnp.mean(rows * rows, axis=-1, keepdims=True) + norm_eps)
    return rows * inverse, inverse


def fill_window(second, first, own, keys, values):
    tokens = own.shape[1]
    for n, part in enumerate((second, first, own)):
        keys[n * tokens : (n + 1) * tokens, :] = part[0]
        values[n * tokens : (n + 1) * tokens, :] = part[1]


def forward_kernel(
    seq_ref, q_ref, second, first, own, readout_ref,
    raised_ref, inverse_ref, attended_ref, terms_ref, keys, values, query, total,
):
    tokens, reach = q_ref.shape[0], WINDOW_KEYS + TILE
    fill_window(second, first, own, keys, values)
    for g in range(2):
        unit, _ = unit_of(q_ref[:, g * HEAD_SIZE : (g + 1) * HEAD_SIZE])
        query[g] = (unit * (score_scale * LOG2_E)).astype(jnp.bfloat16)
    oldest = tokens * jnp.maximum(2 - seq_ref[0], 0)
    row = lax.broadcasted_iota(jnp.int32, (2 * TILE, TILE), 0) % TILE
    column = lax.broadcasted_iota(jnp.int32, (2 * TILE, TILE), 1)
    newer = (column > row).astype(jnp.float32)
    older = (column <= row).astype(jnp.float32)

    def tile(t, _):
        at = pl.multiple_of(t * TILE, TILE)
        window = pl.ds(at, reach)
        rows = pl.ds(at, TILE)
        both = jnp.concatenate([query[0, rows, :], query[1, rows, :]], axis=0)
        place = at + lax.broadcasted_iota(jnp.int32, (1, reach), 1)
        seen = (place >= oldest).astype(jnp.float32)
        raised = jnp.exp2(dot(both, keys[window, :], (1, 1))) * seen
        raised = jnp.concatenate(
            [raised[:, :TILE] * newer, raised[:, TILE:-TILE], raised[:, -TILE:] * older], axis=1
        )
        inverse = 1.0 / jnp.sum(raised, axis=-1, keepdims=True)
        kept = raised.astype(jnp.bfloat16)
        attended = (dot(kept, values[window, :], (1, 0)) * inverse).astype(jnp.bfloat16)
        for g in range(2):
            raised_ref[g, rows, :] = kept[g * TILE : (g + 1) * TILE]
            inverse_ref[g, rows, :] = inverse[g * TILE : (g + 1) * TILE]
            attended_ref[rows, g * HEAD_SIZE : (g + 1) * HEAD_SIZE] = attended[
                g * TILE : (g + 1) * TILE
            ]
        return 0

    lax.fori_loop(0, tokens // TILE, tile, 0)
    term = dot(attended_ref[...], readout_ref[...], (1, 0))

    @pl.when(pl.program_id(0) == 0)
    def _():
        total[...] = term

    @pl.when(pl.program_id(0) == 1)
    def _():
        terms_ref[...] = (total[...] + term).astype(jnp.bfloat16)


def backward_kernel(
    dlogits_ref, readout_ref, q_ref, raised_ref, inverse_ref, attended_ref, second, first, own,
    q_grad_ref, to_second, to_first, to_own,
    keys, values, query, upstream, key_sum, value_sum,
):
    tokens, reach = q_ref.shape[0], WINDOW_KEYS + TILE
    fill_window(second, first, own, keys, values)
    for g in range(2):
        unit, _ = unit_of(q_ref[:, g * HEAD_SIZE : (g + 1) * HEAD_SIZE])
        query[g] = unit.astype(jnp.bfloat16)
    upstream[...] = dot(dlogits_ref[...], readout_ref[...], (1, 1))
    key_sum[...] = jnp.zeros_like(key_sum)
    value_sum[...] = jnp.zeros_like(value_sum)

    def tile(t, _):
        at = pl.multiple_of(t * TILE, TILE)
        window = pl.ds(at, reach)
        rows = pl.ds(at, TILE)
        scaled, offset = [], []
        for g in range(2):
            columns = slice(g * HEAD_SIZE, (g + 1) * HEAD_SIZE)
            grad = upstream[rows, columns] * inverse_ref[g, rows, :]
            offset.append(
                jnp.sum(grad * attended_ref[rows, columns].astype(jnp.float32), axis=-1, keepdims=True)
            )
            scaled.append(grad.astype(jnp.bfloat16))
        scaled = jnp.concatenate(scaled, axis=0)
        offset = jnp.concatenate(offset, axis=0)
        raised = jnp.concatenate([raised_ref[0, rows, :], raised_ref[1, rows, :]], axis=0)
        both = jnp.concatenate([query[0, rows, :], query[1, rows, :]], axis=0)
        weights = dot(scaled, values[window, :], (1, 1))
        scores = (raised.astype(jnp.float32) * (weights - offset)).astype(jnp.bfloat16)
        value_sum[window, :] += dot(raised, scaled, (0, 0))
        key_sum[window, :] += dot(scores, both, (0, 0))
        hat = dot(scores, keys[window, :], (1, 0)) * score_scale
        for g in range(2):
            columns = slice(g * HEAD_SIZE, (g + 1) * HEAD_SIZE)
            unit, inverse = unit_of(q_ref[rows, columns])
            part = hat[g * TILE : (g + 1) * TILE]
            q_grad_ref[rows, columns] = inverse * (
                part - unit * jnp.mean(unit * part, axis=-1, keepdims=True)
            )
        return 0

    lax.fori_loop(0, tokens // TILE, tile, 0)
    for n, out in enumerate((to_second, to_first, to_own)):
        part = slice(n * tokens, (n + 1) * tokens)
        out[0] = (key_sum[part, :] * score_scale).astype(out.dtype)
        out[1] = value_sum[part, :].astype(out.dtype)


def window_specs(tokens):
    return [pl.BlockSpec((2, tokens, HEAD_SIZE), lambda k: (0, 0, k))] * 3


def attention_forward(seq, queries, second, first, own, readout):
    tokens, width = queries.shape
    kv_heads, reach = own.shape[2] // HEAD_SIZE, WINDOW_KEYS + TILE
    candidates = readout.shape[1]
    return pl.pallas_call(
        forward_kernel,
        grid=(kv_heads,),
        in_specs=[
            pl.BlockSpec(memory_space=pltpu.SMEM),
            pl.BlockSpec((tokens, 2 * HEAD_SIZE), lambda k: (0, k)),
            *window_specs(tokens),
            pl.BlockSpec((2 * HEAD_SIZE, candidates), lambda k: (k, 0)),
        ],
        out_specs=[
            pl.BlockSpec((2, tokens, reach), lambda k: (k, 0, 0)),
            pl.BlockSpec((2, tokens, 1), lambda k: (k, 0, 0)),
            pl.BlockSpec((tokens, 2 * HEAD_SIZE), lambda k: (0, k)),
            pl.BlockSpec((tokens, candidates), lambda k: (0, 0)),
        ],
        out_shape=[
            jax.ShapeDtypeStruct((2 * kv_heads, tokens, reach), jnp.bfloat16),
            jax.ShapeDtypeStruct((2 * kv_heads, tokens, 1), jnp.float32),
            jax.ShapeDtypeStruct((tokens, width), jnp.bfloat16),
            jax.ShapeDtypeStruct((tokens, candidates), jnp.bfloat16),
        ],
        scratch_shapes=[
            pltpu.VMEM((3 * tokens, HEAD_SIZE), jnp.bfloat16),
            pltpu.VMEM((3 * tokens, HEAD_SIZE), jnp.bfloat16),
            pltpu.VMEM((2, tokens, HEAD_SIZE), jnp.bfloat16),
            pltpu.VMEM((tokens, candidates), jnp.float32),
        ],
        compiler_params=pltpu.CompilerParams(
            dimension_semantics=("arbitrary",), vmem_limit_bytes=32 << 20
        ),
        cost_estimate=pl.CostEstimate(
            flops=2_500_000_000, bytes_accessed=8_000_000, transcendentals=2_400_000
        ),
        name="attention_forward",
    )(seq.reshape(1), queries, second, first, own, readout)


def attention_backward(dlogits, readout, queries, raised, inverse, attended, second, first, own):
    tokens, width = queries.shape
    kv_heads, reach = own.shape[2] // HEAD_SIZE, WINDOW_KEYS + TILE
    candidates = readout.shape[1]
    pair = pl.BlockSpec((tokens, 2 * HEAD_SIZE), lambda k: (0, k))
    return pl.pallas_call(
        backward_kernel,
        grid=(kv_heads,),
        in_specs=[
            pl.BlockSpec((tokens, candidates), lambda k: (0, 0)),
            pl.BlockSpec((2 * HEAD_SIZE, candidates), lambda k: (k, 0)),
            pair,
            pl.BlockSpec((2, tokens, reach), lambda k: (k, 0, 0)),
            pl.BlockSpec((2, tokens, 1), lambda k: (k, 0, 0)),
            pair,
            *window_specs(tokens),
        ],
        out_specs=[pair, *window_specs(tokens)],
        out_shape=[
            jax.ShapeDtypeStruct((tokens, width), jnp.float32),
            jax.ShapeDtypeStruct(own.shape, jnp.bfloat16),
            jax.ShapeDtypeStruct(own.shape, jnp.bfloat16),
            jax.ShapeDtypeStruct(own.shape, jnp.float32),
        ],
        scratch_shapes=[
            pltpu.VMEM((3 * tokens, HEAD_SIZE), jnp.bfloat16),
            pltpu.VMEM((3 * tokens, HEAD_SIZE), jnp.bfloat16),
            pltpu.VMEM((2, tokens, HEAD_SIZE), jnp.bfloat16),
            pltpu.VMEM((tokens, 2 * HEAD_SIZE), jnp.float32),
            pltpu.VMEM((3 * tokens, HEAD_SIZE), jnp.float32),
            pltpu.VMEM((3 * tokens, HEAD_SIZE), jnp.float32),
        ],
        compiler_params=pltpu.CompilerParams(
            dimension_semantics=("arbitrary",), vmem_limit_bytes=40 << 20
        ),
        cost_estimate=pl.CostEstimate(
            flops=5_000_000_000, bytes_accessed=12_000_000, transcendentals=0
        ),
        name="attention_backward",
    )(dlogits, readout, queries, raised, inverse, attended, second, first, own)


def normalized_rows(value_rows):
    inverse = lax.rsqrt(jnp.mean(value_rows * value_rows, axis=-1, keepdims=True) + norm_eps)
    return (value_rows * inverse, inverse)


def unit_norm_backward(unit, inverse, upstream):
    return inverse * (upstream - unit * jnp.mean(unit * upstream, axis=-1, keepdims=True))


def shards(inputs, queries, key_matrix, value_matrix, readout, token_mask, targets):
    tokens = inputs.shape[0]
    kv_width = key_matrix.shape[1]
    kv_heads = kv_width // HEAD_SIZE
    heads = lax.axis_size("head")
    seq = lax.axis_index("seq")
    core = seq % CORES
    own_weight = jnp.concatenate([key_matrix, value_matrix], axis=1)
    full_weight = gathered_weights(own_weight)
    own_weight, _ = lax.optimization_barrier((own_weight, full_weight[:8, :128]))
    rows_weight = weight_rows(own_weight)
    projected = jnp.dot(inputs, full_weight, preferred_element_type=jnp.float32)
    key_unscaled = projected[:, :kv_width].reshape(tokens, kv_heads, HEAD_SIZE)
    key_unit_rows, key_inverse_norm = normalized_rows(key_unscaled)
    key_normalized_rows = key_unit_rows.astype(jnp.bfloat16)
    paired = jnp.stack([key_normalized_rows.reshape(tokens, kv_width), projected[:, kv_width:].astype(jnp.bfloat16)])
    second = along(paired, 2)
    first = lax.ppermute(jnp.where(core == 0, paired, second), "seq", CORE_SWAP)
    raised, inverse, attended, partial_value = attention_forward(
        seq, queries, second, first, paired, readout
    )

    share = tokens // heads
    terms = lax.all_to_all(partial_value, "head", 0, 0, tiled=True)
    logits = jnp.sum(terms.astype(jnp.float32).reshape(heads, share, -1), axis=0)
    mine = lax.axis_index("head") * share
    wanted = lax.dynamic_slice_in_dim(targets, mine, share, 0)
    chosen = lax.dynamic_slice_in_dim(token_mask, mine, share, 0).astype(jnp.float32)[:, None]
    capped = softcap * jnp.tanh(logits / softcap)
    expo = jnp.exp(capped)
    probs = expo / jnp.sum(expo, axis=-1, keepdims=True)
    onehot = (wanted[:, None] == jnp.arange(logits.shape[1], dtype=jnp.int32)[None, :]).astype(
        jnp.float32
    )
    dlogits = (chosen * (probs - onehot) * (1.0 - (capped / softcap) ** 2)).astype(jnp.bfloat16)
    dlogits = lax.all_to_all(
        jnp.broadcast_to(dlogits[None], (heads,) + dlogits.shape), "head", 0, 0, tiled=True
    ).reshape(tokens, -1)

    query_grad, to_second, to_first, total = attention_backward(
        dlogits, readout, queries, raised, inverse, attended, second, first, paired
    )
    crossed = lax.ppermute(to_first, "seq", CORE_SWAP).astype(jnp.float32)
    outgoing = to_second.astype(jnp.float32) + jnp.where(core == 1, crossed, 0.0)
    arrived = along(outgoing.astype(jnp.bfloat16), -2).astype(jnp.float32)
    total = total + arrived + jnp.where(core == 0, crossed, 0.0)
    key_gradient = unit_norm_backward(
        key_unit_rows, key_inverse_norm, total[0].reshape(tokens, kv_heads, HEAD_SIZE)
    )
    both_grad = jnp.concatenate(
        [key_gradient.reshape(tokens, kv_width), total[1]], axis=1
    ).astype(jnp.bfloat16)
    input_grad = head_product(rows_weight, both_grad).T
    return (query_grad, input_grad)


def solution(mesh):
    in_specs = (
        P("seq", None),
        P("seq", "head"),
        P("seq", "head"),
        P("seq", "head"),
        P("head", None),
        P("seq"),
        P("seq"),
    )
    out_specs = (P("seq", "head"), P("seq", "head"))
    return jax.shard_map(shards, mesh=mesh, in_specs=in_specs, out_specs=out_specs, check_vma=False)
```

```python
import jax
import jax.numpy as jnp
from jax import lax
from jax.experimental import pallas as pl
from jax.experimental.pallas import tpu as pltpu
from jax.sharding import PartitionSpec as P

HEAD_SIZE = 128
WINDOW_KEYS = 1024

norm_eps = 1e-06
softcap = 30.0
score_scale = 168.0 ** (-0.5)
LOG2_E = 1.4426950408889634

Y_LO, Z, CORES = 2, 8, 2
Y_HI, X = 2, 4


def seq_pairs(move):
    pairs = []
    for y in range(Y_LO):
        for z in range(Z):
            for c in range(CORES):
                ty, tz, tc = move(y, z, c)
                pairs.append(((y * Z + z) * CORES + c, (ty * Z + tz) * CORES + tc))
    return pairs


CORE_SWAP = seq_pairs(lambda y, z, c: (y, z, 1 - c))
Y_SWAP = seq_pairs(lambda y, z, c: (1 - y, z, c))
Z_UP = seq_pairs(lambda y, z, c: (y, (z + 1) % Z, c))
Z_DOWN = seq_pairs(lambda y, z, c: (y, (z - 1) % Z, c))


def head_pairs(flip, steps):
    return [
        (y * X + x, (y ^ flip) * X + (x + steps) % X) for y in range(Y_HI) for x in range(X)
    ]


X_UP, X_DOWN, Y_HI_SWAP = head_pairs(0, 1), head_pairs(0, -1), head_pairs(1, 0)


def after(value, *others):
    for other in others:
        corner = other[(slice(0, 1),) * other.ndim].reshape((1,) * value.ndim)
        value = value + (corner * 0).astype(value.dtype)
    return value


class RowsGather:
    def __init__(self, own):
        heads, per_head = Y_HI * X, Y_LO * Z * CORES // (Y_HI * X)
        pairs = [
            ((per_head * h + r) * heads + g, (per_head * g + r) * heads + h)
            for h in range(heads)
            for r in range(per_head)
            for g in range(heads)
        ]
        self.own = lax.ppermute(own, ("seq", "head"), pairs)

    def pair(self, *others):
        seq = lax.axis_index("seq")
        y = seq // (Z * CORES)
        other = lax.ppermute(after(self.own, *others), "seq", Y_SWAP)
        self.up = self.down = jnp.stack(
            [jnp.where(y == 0, self.own, other), jnp.where(y == 0, other, self.own)]
        )
        self.blocks = {0: self.up}

    def hop(self, k, *others):
        up, down = after(self.up, *others), after(self.down, *others)
        if k < Z // 2:
            self.up = lax.ppermute(up, "seq", Z_UP)
            self.down = lax.ppermute(down, "seq", Z_DOWN)
            self.blocks[-k], self.blocks[k] = self.up, self.down
        else:
            self.blocks[k] = lax.ppermute(up, "seq", Z_UP)

    def finish(self, *others):
        seq = lax.axis_index("seq")
        z, core = (seq // CORES) % Z, seq % CORES
        rows, columns = self.own.shape
        full = jnp.zeros((Y_LO, Z, CORES, rows, columns), self.own.dtype)
        mine = jnp.zeros((Y_LO, Z, rows, columns), self.own.dtype)
        for offset, block in self.blocks.items():
            at = jnp.mod(z + offset, Z)
            if offset == Z // 2:
                block = after(block, *others)
            mine = lax.dynamic_update_slice(mine, block[:, None], (0, at, 0, 0))
        theirs = lax.ppermute(mine, "seq", CORE_SWAP)
        for part, c in ((mine, core), (theirs, 1 - core)):
            full = lax.dynamic_update_slice(full, part[:, :, None], (0, 0, c, 0, 0))
        return full.reshape(Y_HI * X, -1, columns)


def head_product(weight, own):
    head = lax.axis_index("head")
    y, x = head // X, head % X

    def send(value, pairs):
        return lax.ppermute(value, "head", pairs)

    def term(value, flip, steps):
        block = lax.dynamic_index_in_dim(
            weight, (y ^ flip) * X + jnp.mod(x - steps, X), 0, keepdims=False
        )
        return lax.dot_general(
            block, value, (((1,), (1,)), ((), ())), preferred_element_type=jnp.float32
        )

    half = own.shape[0] // 2
    below, above, across = send(own, X_UP), send(own, X_DOWN), send(own, Y_HI_SWAP)
    far = jnp.concatenate([send(below[:half], X_UP), send(above[half:], X_DOWN)])
    across_below, across_above = send(across, X_UP), send(across, X_DOWN)
    across_far = send(far, Y_HI_SWAP)
    total = term(own, 0, 0)
    for value, flip, steps in (
        (below, 0, 1),
        (above, 0, -1),
        (across, 1, 0),
        (far, 0, 2),
        (across_below, 1, 1),
        (across_above, 1, -1),
        (across_far, 1, 2),
    ):
        total = total + term(value, flip, steps)
    return total


def along(value, steps):
    count = lax.axis_size("seq")
    first, last = max(0, -steps), min(count, count - steps)
    return lax.ppermute(value, "seq", [(i, i + steps) for i in range(first, last)])


def gathered_weights(own):
    rows, columns = own.shape
    seq = lax.axis_index("seq")
    y, z, core = seq // (Z * CORES), (seq // CORES) % Z, seq % CORES
    other = lax.ppermute(own, "seq", Y_SWAP)
    low = jnp.where(y == 0, own, other)
    high = jnp.where(y == 0, other, own)
    pair = jnp.stack([low, high])
    full = jnp.zeros((Y_LO, Z, CORES, rows, columns), own.dtype)

    def put(full, blocks):
        offsets = list(blocks)
        swapped = lax.ppermute(jnp.concatenate(list(blocks.values())), "seq", CORE_SWAP)
        for n, offset in enumerate(offsets):
            at = jnp.mod(z + offset, Z)
            for piece, c in ((blocks[offset], core), (swapped[2 * n : 2 * n + 2], 1 - core)):
                full = lax.dynamic_update_slice(full, piece[:, None, None], (0, at, c, 0, 0))
        return full

    up = down = pair
    near = {0: pair}
    for k in range(1, Z // 2):
        up = lax.ppermute(up, "seq", Z_UP)
        down = lax.ppermute(down, "seq", Z_DOWN)
        near.update({-k: up, k: down})
        if k >= 2:
            full = put(full, near)
            near = {}
    last = jnp.stack(
        [lax.ppermute(up[0], "seq", Z_UP), lax.ppermute(down[1], "seq", Z_DOWN)]
    )
    full = put(full, {Z // 2: last})
    return full.reshape(Y_LO * Z * CORES * rows, columns)


TILE = 128


def dot(a, b, contract):
    return lax.dot_general(a, b, ((contract[:1], contract[1:]), ((), ())), preferred_element_type=jnp.float32)


def unit_of(rows):
    rows = rows.astype(jnp.float32)
    inverse = lax.rsqrt(jnp.mean(rows * rows, axis=-1, keepdims=True) + norm_eps)
    return rows * inverse, inverse


def fill_window(second, first, own, keys, values):
    tokens = own.shape[1]
    for n, part in enumerate((second, first, own)):
        keys[n * tokens : (n + 1) * tokens, :] = part[0]
        values[n * tokens : (n + 1) * tokens, :] = part[1]


def forward_kernel(
    seq_ref, q_ref, second, first, own, readout_ref,
    raised_ref, inverse_ref, attended_ref, terms_ref, keys, values, query, total,
):
    tokens, reach = q_ref.shape[0], WINDOW_KEYS + TILE
    fill_window(second, first, own, keys, values)
    for g in range(2):
        unit, _ = unit_of(q_ref[:, g * HEAD_SIZE : (g + 1) * HEAD_SIZE])
        query[g] = (unit * (score_scale * LOG2_E)).astype(jnp.bfloat16)
    oldest = tokens * jnp.maximum(2 - seq_ref[0], 0)
    row = lax.broadcasted_iota(jnp.int32, (2 * TILE, TILE), 0) % TILE
    column = lax.broadcasted_iota(jnp.int32, (2 * TILE, TILE), 1)
    newer = (column > row).astype(jnp.float32)
    older = (column <= row).astype(jnp.float32)

    def tile(t, _):
        at = pl.multiple_of(t * TILE, TILE)
        window = pl.ds(at, reach)
        rows = pl.ds(at, TILE)
        both = jnp.concatenate([query[0, rows, :], query[1, rows, :]], axis=0)
        place = at + lax.broadcasted_iota(jnp.int32, (1, reach), 1)
        seen = (place >= oldest).astype(jnp.float32)
        raised = jnp.exp2(dot(both, keys[window, :], (1, 1))) * seen
        raised = jnp.concatenate(
            [raised[:, :TILE] * newer, raised[:, TILE:-TILE], raised[:, -TILE:] * older], axis=1
        )
        inverse = 1.0 / jnp.sum(raised, axis=-1, keepdims=True)
        kept = raised.astype(jnp.bfloat16)
        attended = (dot(kept, values[window, :], (1, 0)) * inverse).astype(jnp.bfloat16)
        for g in range(2):
            raised_ref[g, rows, :] = kept[g * TILE : (g + 1) * TILE]
            inverse_ref[g, rows, :] = inverse[g * TILE : (g + 1) * TILE]
            attended_ref[rows, g * HEAD_SIZE : (g + 1) * HEAD_SIZE] = attended[
                g * TILE : (g + 1) * TILE
            ]
        return 0

    lax.fori_loop(0, tokens // TILE, tile, 0)
    term = dot(attended_ref[...], readout_ref[...], (1, 0))

    @pl.when(pl.program_id(0) == 0)
    def _():
        total[...] = term

    @pl.when(pl.program_id(0) == 1)
    def _():
        terms_ref[...] = (total[...] + term).astype(jnp.bfloat16)


def backward_kernel(
    dlogits_ref, readout_ref, q_ref, raised_ref, inverse_ref, attended_ref, second, first, own,
    q_grad_ref, to_second, to_first, to_own,
    keys, values, query, upstream, key_sum, value_sum,
):
    tokens, reach = q_ref.shape[0], WINDOW_KEYS + TILE
    fill_window(second, first, own, keys, values)
    for g in range(2):
        unit, _ = unit_of(q_ref[:, g * HEAD_SIZE : (g + 1) * HEAD_SIZE])
        query[g] = unit.astype(jnp.bfloat16)
    upstream[...] = dot(dlogits_ref[...], readout_ref[...], (1, 1))
    key_sum[...] = jnp.zeros_like(key_sum)
    value_sum[...] = jnp.zeros_like(value_sum)

    def tile(t, _):
        at = pl.multiple_of(t * TILE, TILE)
        window = pl.ds(at, reach)
        rows = pl.ds(at, TILE)
        scaled, offset = [], []
        for g in range(2):
            columns = slice(g * HEAD_SIZE, (g + 1) * HEAD_SIZE)
            grad = upstream[rows, columns] * inverse_ref[g, rows, :]
            offset.append(
                jnp.sum(grad * attended_ref[rows, columns].astype(jnp.float32), axis=-1, keepdims=True)
            )
            scaled.append(grad.astype(jnp.bfloat16))
        scaled = jnp.concatenate(scaled, axis=0)
        offset = jnp.concatenate(offset, axis=0)
        raised = jnp.concatenate([raised_ref[0, rows, :], raised_ref[1, rows, :]], axis=0)
        both = jnp.concatenate([query[0, rows, :], query[1, rows, :]], axis=0)
        weights = dot(scaled, values[window, :], (1, 1))
        scores = (raised.astype(jnp.float32) * (weights - offset)).astype(jnp.bfloat16)
        value_sum[window, :] += dot(raised, scaled, (0, 0))
        key_sum[window, :] += dot(scores, both, (0, 0))
        hat = dot(scores, keys[window, :], (1, 0)) * score_scale
        for g in range(2):
            columns = slice(g * HEAD_SIZE, (g + 1) * HEAD_SIZE)
            unit, inverse = unit_of(q_ref[rows, columns])
            part = hat[g * TILE : (g + 1) * TILE]
            q_grad_ref[rows, columns] = inverse * (
                part - unit * jnp.mean(unit * part, axis=-1, keepdims=True)
            )
        return 0

    lax.fori_loop(0, tokens // TILE, tile, 0)
    for n, out in enumerate((to_second, to_first, to_own)):
        part = slice(n * tokens, (n + 1) * tokens)
        out[0] = (key_sum[part, :] * score_scale).astype(out.dtype)
        out[1] = value_sum[part, :].astype(out.dtype)


def window_specs(tokens):
    return [pl.BlockSpec((2, tokens, HEAD_SIZE), lambda k: (0, 0, k))] * 3


def attention_forward(seq, queries, second, first, own, readout):
    tokens, width = queries.shape
    kv_heads, reach = own.shape[2] // HEAD_SIZE, WINDOW_KEYS + TILE
    candidates = readout.shape[1]
    return pl.pallas_call(
        forward_kernel,
        grid=(kv_heads,),
        in_specs=[
            pl.BlockSpec(memory_space=pltpu.SMEM),
            pl.BlockSpec((tokens, 2 * HEAD_SIZE), lambda k: (0, k)),
            *window_specs(tokens),
            pl.BlockSpec((2 * HEAD_SIZE, candidates), lambda k: (k, 0)),
        ],
        out_specs=[
            pl.BlockSpec((2, tokens, reach), lambda k: (k, 0, 0)),
            pl.BlockSpec((2, tokens, 1), lambda k: (k, 0, 0)),
            pl.BlockSpec((tokens, 2 * HEAD_SIZE), lambda k: (0, k)),
            pl.BlockSpec((tokens, candidates), lambda k: (0, 0)),
        ],
        out_shape=[
            jax.ShapeDtypeStruct((2 * kv_heads, tokens, reach), jnp.bfloat16),
            jax.ShapeDtypeStruct((2 * kv_heads, tokens, 1), jnp.float32),
            jax.ShapeDtypeStruct((tokens, width), jnp.bfloat16),
            jax.ShapeDtypeStruct((tokens, candidates), jnp.bfloat16),
        ],
        scratch_shapes=[
            pltpu.VMEM((3 * tokens, HEAD_SIZE), jnp.bfloat16),
            pltpu.VMEM((3 * tokens, HEAD_SIZE), jnp.bfloat16),
            pltpu.VMEM((2, tokens, HEAD_SIZE), jnp.bfloat16),
            pltpu.VMEM((tokens, candidates), jnp.float32),
        ],
        compiler_params=pltpu.CompilerParams(dimension_semantics=("arbitrary",)),
        cost_estimate=pl.CostEstimate(
            flops=2_500_000_000, bytes_accessed=8_000_000, transcendentals=2_400_000
        ),
        name="attention_forward",
    )(seq.reshape(1), queries, second, first, own, readout)


def attention_backward(dlogits, readout, queries, raised, inverse, attended, second, first, own):
    tokens, width = queries.shape
    kv_heads, reach = own.shape[2] // HEAD_SIZE, WINDOW_KEYS + TILE
    candidates = readout.shape[1]
    pair = pl.BlockSpec((tokens, 2 * HEAD_SIZE), lambda k: (0, k))
    return pl.pallas_call(
        backward_kernel,
        grid=(kv_heads,),
        in_specs=[
            pl.BlockSpec((tokens, candidates), lambda k: (0, 0)),
            pl.BlockSpec((2 * HEAD_SIZE, candidates), lambda k: (k, 0)),
            pair,
            pl.BlockSpec((2, tokens, reach), lambda k: (k, 0, 0)),
            pl.BlockSpec((2, tokens, 1), lambda k: (k, 0, 0)),
            pair,
            *window_specs(tokens),
        ],
        out_specs=[pair, *window_specs(tokens)],
        out_shape=[
            jax.ShapeDtypeStruct((tokens, width), jnp.float32),
            jax.ShapeDtypeStruct(own.shape, jnp.bfloat16),
            jax.ShapeDtypeStruct(own.shape, jnp.bfloat16),
            jax.ShapeDtypeStruct(own.shape, jnp.float32),
        ],
        scratch_shapes=[
            pltpu.VMEM((3 * tokens, HEAD_SIZE), jnp.bfloat16),
            pltpu.VMEM((3 * tokens, HEAD_SIZE), jnp.bfloat16),
            pltpu.VMEM((2, tokens, HEAD_SIZE), jnp.bfloat16),
            pltpu.VMEM((tokens, 2 * HEAD_SIZE), jnp.float32),
            pltpu.VMEM((3 * tokens, HEAD_SIZE), jnp.float32),
            pltpu.VMEM((3 * tokens, HEAD_SIZE), jnp.float32),
        ],
        compiler_params=pltpu.CompilerParams(dimension_semantics=("arbitrary",)),
        cost_estimate=pl.CostEstimate(
            flops=5_000_000_000, bytes_accessed=12_000_000, transcendentals=0
        ),
        name="attention_backward",
    )(dlogits, readout, queries, raised, inverse, attended, second, first, own)


def normalized_rows(value_rows):
    inverse = lax.rsqrt(jnp.mean(value_rows * value_rows, axis=-1, keepdims=True) + norm_eps)
    return (value_rows * inverse, inverse)


def unit_norm_backward(unit, inverse, upstream):
    return inverse * (upstream - unit * jnp.mean(unit * upstream, axis=-1, keepdims=True))


def shards(inputs, queries, key_matrix, value_matrix, readout, token_mask, targets):
    tokens = inputs.shape[0]
    kv_width = key_matrix.shape[1]
    kv_heads = kv_width // HEAD_SIZE
    heads = lax.axis_size("head")
    seq = lax.axis_index("seq")
    core = seq % CORES
    own_weight = jnp.concatenate([key_matrix, value_matrix], axis=1)
    full_weight = gathered_weights(own_weight)
    rows_gather = RowsGather(own_weight)
    projected = jnp.dot(inputs, full_weight, preferred_element_type=jnp.float32)
    key_unscaled = projected[:, :kv_width].reshape(tokens, kv_heads, HEAD_SIZE)
    key_unit_rows, key_inverse_norm = normalized_rows(key_unscaled)
    key_normalized_rows = key_unit_rows.astype(jnp.bfloat16)
    paired = jnp.stack([key_normalized_rows.reshape(tokens, kv_width), projected[:, kv_width:].astype(jnp.bfloat16)])
    second = along(paired, 2)
    first = lax.ppermute(jnp.where(core == 0, paired, second), "seq", CORE_SWAP)
    rows_gather.pair(paired)
    rows_gather.hop(1, second)
    raised, inverse, attended, partial_value = attention_forward(
        seq, queries, second, first, paired, readout
    )

    share = tokens // heads
    terms = lax.all_to_all(partial_value, "head", 0, 0, tiled=True)
    rows_gather.hop(2, partial_value)
    logits = jnp.sum(terms.astype(jnp.float32).reshape(heads, share, -1), axis=0)
    mine = lax.axis_index("head") * share
    wanted = lax.dynamic_slice_in_dim(targets, mine, share, 0)
    chosen = lax.dynamic_slice_in_dim(token_mask, mine, share, 0).astype(jnp.float32)[:, None]
    capped = softcap * jnp.tanh(logits / softcap)
    expo = jnp.exp(capped)
    probs = expo / jnp.sum(expo, axis=-1, keepdims=True)
    onehot = (wanted[:, None] == jnp.arange(logits.shape[1], dtype=jnp.int32)[None, :]).astype(
        jnp.float32
    )
    dlogits = (chosen * (probs - onehot) * (1.0 - (capped / softcap) ** 2)).astype(jnp.bfloat16)
    rows_gather.hop(3, dlogits)
    dlogits = lax.all_to_all(
        jnp.broadcast_to(dlogits[None], (heads,) + dlogits.shape), "head", 0, 0, tiled=True
    ).reshape(tokens, -1)

    dlogits = after(dlogits, rows_gather.up, rows_gather.down)
    rows_gather.hop(4)
    query_grad, to_second, to_first, total = attention_backward(
        dlogits, readout, queries, raised, inverse, attended, second, first, paired
    )
    crossed = lax.ppermute(to_first, "seq", CORE_SWAP).astype(jnp.float32)
    outgoing = to_second.astype(jnp.float32) + jnp.where(core == 1, crossed, 0.0)
    outgoing = outgoing.astype(jnp.bfloat16)
    arrived = along(outgoing, -2).astype(jnp.float32)
    rows_weight = rows_gather.finish(outgoing)
    total = total + arrived + jnp.where(core == 0, crossed, 0.0)
    key_gradient = unit_norm_backward(
        key_unit_rows, key_inverse_norm, total[0].reshape(tokens, kv_heads, HEAD_SIZE)
    )
    both_grad = jnp.concatenate(
        [key_gradient.reshape(tokens, kv_width), total[1]], axis=1
    ).astype(jnp.bfloat16)
    input_grad = head_product(rows_weight, both_grad).T
    return (query_grad, input_grad)


def solution(mesh):
    in_specs = (
        P("seq", None),
        P("seq", "head"),
        P("seq", "head"),
        P("seq", "head"),
        P("head", None),
        P("seq"),
        P("seq"),
    )
    out_specs = (P("seq", "head"), P("seq", "head"))
    return jax.shard_map(shards, mesh=mesh, in_specs=in_specs, out_specs=out_specs, check_vma=False)
```

```python
import jax
import jax.numpy as jnp
from jax import lax
from jax.experimental import pallas as pl
from jax.experimental.pallas import tpu as pltpu
from jax.sharding import PartitionSpec as P

HEAD_SIZE = 128
WINDOW_KEYS = 1024

norm_eps = 1e-06
softcap = 30.0
score_scale = 168.0 ** (-0.5)
LOG2_E = 1.4426950408889634

Y_LO, Z, CORES = 2, 8, 2
Y_HI, X = 2, 4


def seq_pairs(move):
    pairs = []
    for y in range(Y_LO):
        for z in range(Z):
            for c in range(CORES):
                ty, tz, tc = move(y, z, c)
                pairs.append(((y * Z + z) * CORES + c, (ty * Z + tz) * CORES + tc))
    return pairs


CORE_SWAP = seq_pairs(lambda y, z, c: (y, z, 1 - c))
Y_SWAP = seq_pairs(lambda y, z, c: (1 - y, z, c))
Z_UP = seq_pairs(lambda y, z, c: (y, (z + 1) % Z, c))
Z_DOWN = seq_pairs(lambda y, z, c: (y, (z - 1) % Z, c))


def head_pairs(flip, steps):
    return [
        (y * X + x, (y ^ flip) * X + (x + steps) % X) for y in range(Y_HI) for x in range(X)
    ]


X_UP, X_DOWN, Y_HI_SWAP = head_pairs(0, 1), head_pairs(0, -1), head_pairs(1, 0)


def after(value, other):
    corner = other[(slice(0, 1),) * other.ndim].reshape((1,) * value.ndim)
    return value + (corner * 0).astype(value.dtype)


def moved_to_head(own):
    heads = Y_HI * X
    pairs = []
    for y in range(Y_HI):
        for x in range(X):
            for p in range(Y_HI):
                for q in range(X):
                    for low in range(2):
                        for core in range(CORES):
                            source = (y * Z + 2 * x + low) * CORES + core
                            target = (p * Z + (2 * (x + q) + low) % Z) * CORES + core
                            pairs.append((source * heads + p * X + q, target * heads + y * X + x))
    return lax.ppermute(own, ("seq", "head"), pairs)


def gathered_rows(moved):
    columns = moved.shape[1]
    return lax.all_gather(moved, "seq", axis=0, tiled=True).reshape(Y_HI * X, -1, columns)


def head_product(weight, own):
    head = lax.axis_index("head")
    y, x = head // X, head % X

    def send(value, pairs):
        return lax.ppermute(value, "head", pairs)

    def term(value, flip, steps):
        block = lax.dynamic_index_in_dim(
            weight, (y ^ flip) * X + jnp.mod(2 * x - steps, X), 0, keepdims=False
        )
        return lax.dot_general(
            block, value, (((1,), (1,)), ((), ())), preferred_element_type=jnp.float32
        )

    half = own.shape[0] // 2
    below, above, across = send(own, X_UP), send(own, X_DOWN), send(own, Y_HI_SWAP)
    far = jnp.concatenate([send(below[:half], X_UP), send(above[half:], X_DOWN)])
    across_below, across_above = send(across, X_UP), send(across, X_DOWN)
    across_far = send(far, Y_HI_SWAP)
    total = term(own, 0, 0)
    for value, flip, steps in (
        (below, 0, 1),
        (above, 0, -1),
        (across, 1, 0),
        (far, 0, 2),
        (across_below, 1, 1),
        (across_above, 1, -1),
        (across_far, 1, 2),
    ):
        total = total + term(value, flip, steps)
    return total


def along(value, steps):
    count = lax.axis_size("seq")
    first, last = max(0, -steps), min(count, count - steps)
    return lax.ppermute(value, "seq", [(i, i + steps) for i in range(first, last)])


def gathered_weights(own):
    rows, columns = own.shape
    seq = lax.axis_index("seq")
    y, z, core = seq // (Z * CORES), (seq // CORES) % Z, seq % CORES
    other = lax.ppermute(own, "seq", Y_SWAP)
    low = jnp.where(y == 0, own, other)
    high = jnp.where(y == 0, other, own)
    pair = jnp.stack([low, high])
    full = jnp.zeros((Y_LO, Z, CORES, rows, columns), own.dtype)

    def put(full, blocks):
        offsets = list(blocks)
        swapped = lax.ppermute(jnp.concatenate(list(blocks.values())), "seq", CORE_SWAP)
        for n, offset in enumerate(offsets):
            at = jnp.mod(z + offset, Z)
            for piece, c in ((blocks[offset], core), (swapped[2 * n : 2 * n + 2], 1 - core)):
                full = lax.dynamic_update_slice(full, piece[:, None, None], (0, at, c, 0, 0))
        return full

    up = down = pair
    full = put(full, {0: pair})
    for k in range(1, Z // 2):
        up = lax.ppermute(up, "seq", Z_UP)
        down = lax.ppermute(down, "seq", Z_DOWN)
        full = put(full, {-k: up, k: down})
    last = jnp.stack(
        [lax.ppermute(up[0], "seq", Z_UP), lax.ppermute(down[1], "seq", Z_DOWN)]
    )
    full = put(full, {Z // 2: last})
    return full.reshape(Y_LO * Z * CORES * rows, columns)


TILE = 128


def dot(a, b, contract):
    return lax.dot_general(a, b, ((contract[:1], contract[1:]), ((), ())), preferred_element_type=jnp.float32)


def unit_of(rows):
    rows = rows.astype(jnp.float32)
    inverse = lax.rsqrt(jnp.mean(rows * rows, axis=-1, keepdims=True) + norm_eps)
    return rows * inverse, inverse


def fill_window(second, first, own, keys, values):
    tokens = own.shape[1]
    for n, part in enumerate((second, first, own)):
        keys[n * tokens : (n + 1) * tokens, :] = part[0]
        values[n * tokens : (n + 1) * tokens, :] = part[1]


def forward_kernel(
    seq_ref, q_ref, second, first, own, readout_ref,
    raised_ref, inverse_ref, attended_ref, terms_ref, keys, values, query, total,
):
    tokens, reach = q_ref.shape[0], WINDOW_KEYS + TILE
    fill_window(second, first, own, keys, values)
    for g in range(2):
        unit, _ = unit_of(q_ref[:, g * HEAD_SIZE : (g + 1) * HEAD_SIZE])
        query[g] = (unit * (score_scale * LOG2_E)).astype(jnp.bfloat16)
    oldest = tokens * jnp.maximum(2 - seq_ref[0], 0)
    row = lax.broadcasted_iota(jnp.int32, (2 * TILE, TILE), 0) % TILE
    column = lax.broadcasted_iota(jnp.int32, (2 * TILE, TILE), 1)
    newer = (column > row).astype(jnp.float32)
    older = (column <= row).astype(jnp.float32)

    def tile(t, _):
        at = pl.multiple_of(t * TILE, TILE)
        window = pl.ds(at, reach)
        rows = pl.ds(at, TILE)
        both = jnp.concatenate([query[0, rows, :], query[1, rows, :]], axis=0)
        place = at + lax.broadcasted_iota(jnp.int32, (1, reach), 1)
        seen = (place >= oldest).astype(jnp.float32)
        raised = jnp.exp2(dot(both, keys[window, :], (1, 1))) * seen
        raised = jnp.concatenate(
            [raised[:, :TILE] * newer, raised[:, TILE:-TILE], raised[:, -TILE:] * older], axis=1
        )
        inverse = 1.0 / jnp.sum(raised, axis=-1, keepdims=True)
        kept = raised.astype(jnp.bfloat16)
        attended = (dot(kept, values[window, :], (1, 0)) * inverse).astype(jnp.bfloat16)
        for g in range(2):
            raised_ref[g, rows, :] = kept[g * TILE : (g + 1) * TILE]
            inverse_ref[g, rows, :] = inverse[g * TILE : (g + 1) * TILE]
            attended_ref[rows, g * HEAD_SIZE : (g + 1) * HEAD_SIZE] = attended[
                g * TILE : (g + 1) * TILE
            ]
        return 0

    lax.fori_loop(0, tokens // TILE, tile, 0)
    term = dot(attended_ref[...], readout_ref[...], (1, 0))

    @pl.when(pl.program_id(0) == 0)
    def _():
        total[...] = term

    @pl.when(pl.program_id(0) == 1)
    def _():
        terms_ref[...] = (total[...] + term).astype(jnp.bfloat16)


def backward_kernel(
    dlogits_ref, readout_ref, q_ref, raised_ref, inverse_ref, attended_ref, second, first, own,
    q_grad_ref, to_second, to_first, to_own,
    keys, values, query, upstream, key_sum, value_sum,
):
    tokens, reach = q_ref.shape[0], WINDOW_KEYS + TILE
    fill_window(second, first, own, keys, values)
    for g in range(2):
        unit, _ = unit_of(q_ref[:, g * HEAD_SIZE : (g + 1) * HEAD_SIZE])
        query[g] = unit.astype(jnp.bfloat16)
    upstream[...] = dot(dlogits_ref[...], readout_ref[...], (1, 1))
    key_sum[...] = jnp.zeros_like(key_sum)
    value_sum[...] = jnp.zeros_like(value_sum)

    def tile(t, _):
        at = pl.multiple_of(t * TILE, TILE)
        window = pl.ds(at, reach)
        rows = pl.ds(at, TILE)
        scaled, offset = [], []
        for g in range(2):
            columns = slice(g * HEAD_SIZE, (g + 1) * HEAD_SIZE)
            grad = upstream[rows, columns] * inverse_ref[g, rows, :]
            offset.append(
                jnp.sum(grad * attended_ref[rows, columns].astype(jnp.float32), axis=-1, keepdims=True)
            )
            scaled.append(grad.astype(jnp.bfloat16))
        scaled = jnp.concatenate(scaled, axis=0)
        offset = jnp.concatenate(offset, axis=0)
        raised = jnp.concatenate([raised_ref[0, rows, :], raised_ref[1, rows, :]], axis=0)
        both = jnp.concatenate([query[0, rows, :], query[1, rows, :]], axis=0)
        weights = dot(scaled, values[window, :], (1, 1))
        scores = (raised.astype(jnp.float32) * (weights - offset)).astype(jnp.bfloat16)
        value_sum[window, :] += dot(raised, scaled, (0, 0))
        key_sum[window, :] += dot(scores, both, (0, 0))
        hat = dot(scores, keys[window, :], (1, 0)) * score_scale
        for g in range(2):
            columns = slice(g * HEAD_SIZE, (g + 1) * HEAD_SIZE)
            unit, inverse = unit_of(q_ref[rows, columns])
            part = hat[g * TILE : (g + 1) * TILE]
            q_grad_ref[rows, columns] = inverse * (
                part - unit * jnp.mean(unit * part, axis=-1, keepdims=True)
            )
        return 0

    lax.fori_loop(0, tokens // TILE, tile, 0)
    for n, out in enumerate((to_second, to_first, to_own)):
        part = slice(n * tokens, (n + 1) * tokens)
        out[0] = (key_sum[part, :] * score_scale).astype(out.dtype)
        out[1] = value_sum[part, :].astype(out.dtype)


def normalize_kernel(projected_ref, out):
    width = out.shape[2]
    for low in range(0, width, HEAD_SIZE):
        columns = slice(low, low + HEAD_SIZE)
        out[0, :, columns] = unit_of(projected_ref[:, columns])[0].astype(jnp.bfloat16)
    out[1] = projected_ref[:, width:].astype(jnp.bfloat16)


def normalized(projected):
    tokens, width = projected.shape
    return pl.pallas_call(
        normalize_kernel,
        out_shape=jax.ShapeDtypeStruct((2, tokens, width // 2), jnp.bfloat16),
        cost_estimate=pl.CostEstimate(
            flops=2_000_000, bytes_accessed=1_500_000, transcendentals=1024
        ),
        name="normalized",
    )(projected)


def gradients_kernel(seq_ref, projected_ref, own, crossed, arrived, out):
    width = own.shape[2]
    keep = 1.0 - (seq_ref[0] % CORES).astype(jnp.float32)
    for low in range(0, width, HEAD_SIZE):
        columns = slice(low, low + HEAD_SIZE)
        unit, inverse = unit_of(projected_ref[:, columns])
        keys, values = (
            own[n, :, columns]
            + arrived[n, :, columns].astype(jnp.float32)
            + keep * crossed[n, :, columns].astype(jnp.float32)
            for n in range(2)
        )
        keys = inverse * (keys - unit * jnp.mean(unit * keys, axis=-1, keepdims=True))
        out[:, columns] = keys.astype(jnp.bfloat16)
        out[:, width + low : width + low + HEAD_SIZE] = values.astype(jnp.bfloat16)


def projection_gradients(seq, projected, own, crossed, arrived):
    vmem = pl.BlockSpec(memory_space=pltpu.VMEM)
    return pl.pallas_call(
        gradients_kernel,
        in_specs=[pl.BlockSpec(memory_space=pltpu.SMEM), vmem, vmem, vmem, vmem],
        out_specs=vmem,
        out_shape=jax.ShapeDtypeStruct(projected.shape, jnp.bfloat16),
        cost_estimate=pl.CostEstimate(
            flops=4_000_000, bytes_accessed=3_500_000, transcendentals=1024
        ),
        name="projection_gradients",
    )(seq.reshape(1), projected, own, crossed, arrived)


def window_specs(tokens):
    return [pl.BlockSpec((2, tokens, HEAD_SIZE), lambda k: (0, 0, k))] * 3


def attention_forward(seq, queries, second, first, own, readout):
    tokens, width = queries.shape
    kv_heads, reach = own.shape[2] // HEAD_SIZE, WINDOW_KEYS + TILE
    candidates = readout.shape[1]
    return pl.pallas_call(
        forward_kernel,
        grid=(kv_heads,),
        in_specs=[
            pl.BlockSpec(memory_space=pltpu.SMEM),
            pl.BlockSpec((tokens, 2 * HEAD_SIZE), lambda k: (0, k)),
            *window_specs(tokens),
            pl.BlockSpec((2 * HEAD_SIZE, candidates), lambda k: (k, 0)),
        ],
        out_specs=[
            pl.BlockSpec((2, tokens, reach), lambda k: (k, 0, 0)),
            pl.BlockSpec((2, tokens, 1), lambda k: (k, 0, 0)),
            pl.BlockSpec((tokens, 2 * HEAD_SIZE), lambda k: (0, k)),
            pl.BlockSpec((tokens, candidates), lambda k: (0, 0)),
        ],
        out_shape=[
            jax.ShapeDtypeStruct((2 * kv_heads, tokens, reach), jnp.bfloat16),
            jax.ShapeDtypeStruct((2 * kv_heads, tokens, 1), jnp.float32),
            jax.ShapeDtypeStruct((tokens, width), jnp.bfloat16),
            jax.ShapeDtypeStruct((tokens, candidates), jnp.bfloat16),
        ],
        scratch_shapes=[
            pltpu.VMEM((3 * tokens, HEAD_SIZE), jnp.bfloat16),
            pltpu.VMEM((3 * tokens, HEAD_SIZE), jnp.bfloat16),
            pltpu.VMEM((2, tokens, HEAD_SIZE), jnp.bfloat16),
            pltpu.VMEM((tokens, candidates), jnp.float32),
        ],
        compiler_params=pltpu.CompilerParams(dimension_semantics=("arbitrary",)),
        cost_estimate=pl.CostEstimate(
            flops=2_500_000_000, bytes_accessed=8_000_000, transcendentals=2_400_000
        ),
        name="attention_forward",
    )(seq.reshape(1), queries, second, first, own, readout)


def attention_backward(dlogits, readout, queries, raised, inverse, attended, second, first, own):
    tokens, width = queries.shape
    kv_heads, reach = own.shape[2] // HEAD_SIZE, WINDOW_KEYS + TILE
    candidates = readout.shape[1]
    pair = pl.BlockSpec((tokens, 2 * HEAD_SIZE), lambda k: (0, k))
    return pl.pallas_call(
        backward_kernel,
        grid=(kv_heads,),
        in_specs=[
            pl.BlockSpec((tokens, candidates), lambda k: (0, 0)),
            pl.BlockSpec((2 * HEAD_SIZE, candidates), lambda k: (k, 0)),
            pair,
            pl.BlockSpec((2, tokens, reach), lambda k: (k, 0, 0)),
            pl.BlockSpec((2, tokens, 1), lambda k: (k, 0, 0)),
            pair,
            *window_specs(tokens),
        ],
        out_specs=[pair, *window_specs(tokens)],
        out_shape=[
            jax.ShapeDtypeStruct((tokens, width), jnp.float32),
            jax.ShapeDtypeStruct(own.shape, jnp.bfloat16),
            jax.ShapeDtypeStruct(own.shape, jnp.bfloat16),
            jax.ShapeDtypeStruct(own.shape, jnp.float32),
        ],
        scratch_shapes=[
            pltpu.VMEM((3 * tokens, HEAD_SIZE), jnp.bfloat16),
            pltpu.VMEM((3 * tokens, HEAD_SIZE), jnp.bfloat16),
            pltpu.VMEM((2, tokens, HEAD_SIZE), jnp.bfloat16),
            pltpu.VMEM((tokens, 2 * HEAD_SIZE), jnp.float32),
            pltpu.VMEM((3 * tokens, HEAD_SIZE), jnp.float32),
            pltpu.VMEM((3 * tokens, HEAD_SIZE), jnp.float32),
        ],
        compiler_params=pltpu.CompilerParams(dimension_semantics=("arbitrary",)),
        cost_estimate=pl.CostEstimate(
            flops=5_000_000_000, bytes_accessed=12_000_000, transcendentals=0
        ),
        name="attention_backward",
    )(dlogits, readout, queries, raised, inverse, attended, second, first, own)


def shards(inputs, queries, key_matrix, value_matrix, readout, token_mask, targets):
    tokens = inputs.shape[0]
    heads = lax.axis_size("head")
    seq = lax.axis_index("seq")
    core = seq % CORES
    own_weight = jnp.concatenate([key_matrix, value_matrix], axis=1)
    full_weight = gathered_weights(own_weight)
    projected = jnp.dot(inputs, full_weight, preferred_element_type=jnp.float32)
    paired = normalized(projected)
    second = along(paired, 2)
    first = lax.ppermute(jnp.where(core == 0, paired, second), "seq", CORE_SWAP)
    moved = moved_to_head(after(own_weight, second))
    raised, inverse, attended, partial_value = attention_forward(
        seq, queries, second, first, paired, readout
    )

    rows_weight = gathered_rows(after(moved, partial_value))

    share = tokens // heads
    terms = lax.all_to_all(partial_value, "head", 0, 0, tiled=True)
    logits = jnp.sum(terms.astype(jnp.float32).reshape(heads, share, -1), axis=0)
    mine = lax.axis_index("head") * share
    wanted = lax.dynamic_slice_in_dim(targets, mine, share, 0)
    chosen = lax.dynamic_slice_in_dim(token_mask, mine, share, 0).astype(jnp.float32)[:, None]
    capped = softcap * jnp.tanh(logits / softcap)
    expo = jnp.exp(capped)
    probs = expo / jnp.sum(expo, axis=-1, keepdims=True)
    onehot = (wanted[:, None] == jnp.arange(logits.shape[1], dtype=jnp.int32)[None, :]).astype(
        jnp.float32
    )
    dlogits = (chosen * (probs - onehot) * (1.0 - (capped / softcap) ** 2)).astype(jnp.bfloat16)
    dlogits = lax.all_to_all(
        jnp.broadcast_to(dlogits[None], (heads,) + dlogits.shape), "head", 0, 0, tiled=True
    ).reshape(tokens, -1)

    query_grad, to_second, to_first, total = attention_backward(
        dlogits, readout, queries, raised, inverse, attended, second, first, paired
    )
    crossed = lax.ppermute(to_first, "seq", CORE_SWAP)
    outgoing = to_second.astype(jnp.float32) + jnp.where(core == 1, crossed, 0).astype(jnp.float32)
    arrived = along(outgoing.astype(jnp.bfloat16), -2)
    both_grad = projection_gradients(seq, projected, total, crossed, arrived)
    input_grad = head_product(rows_weight, both_grad).T
    return (query_grad, input_grad)


def solution(mesh):
    in_specs = (
        P("seq", None),
        P("seq", "head"),
        P("seq", "head"),
        P("seq", "head"),
        P("head", None),
        P("seq"),
        P("seq"),
    )
    out_specs = (P("seq", "head"), P("seq", "head"))
    return jax.shard_map(shards, mesh=mesh, in_specs=in_specs, out_specs=out_specs, check_vma=False)
```

```python
import jax
import jax.numpy as jnp
from jax import lax
from jax.experimental import pallas as pl
from jax.experimental.pallas import tpu as pltpu
from jax.sharding import PartitionSpec as P

HEAD_SIZE = 128
WINDOW_KEYS = 1024

norm_eps = 1e-06
softcap = 30.0
score_scale = 168.0 ** (-0.5)
LOG2_E = 1.4426950408889634

Y_LO, Z, CORES = 2, 8, 2
Y_HI, X = 2, 4


def seq_pairs(move):
    pairs = []
    for y in range(Y_LO):
        for z in range(Z):
            for c in range(CORES):
                ty, tz, tc = move(y, z, c)
                pairs.append(((y * Z + z) * CORES + c, (ty * Z + tz) * CORES + tc))
    return pairs


CORE_SWAP = seq_pairs(lambda y, z, c: (y, z, 1 - c))
Y_SWAP = seq_pairs(lambda y, z, c: (1 - y, z, c))
Z_UP = seq_pairs(lambda y, z, c: (y, (z + 1) % Z, c))
Z_DOWN = seq_pairs(lambda y, z, c: (y, (z - 1) % Z, c))


def head_pairs(flip, steps):
    return [
        (y * X + x, (y ^ flip) * X + (x + steps) % X) for y in range(Y_HI) for x in range(X)
    ]


X_UP, X_DOWN, Y_HI_SWAP = head_pairs(0, 1), head_pairs(0, -1), head_pairs(1, 0)


def after(value, other):
    corner = other[(slice(0, 1),) * other.ndim].reshape((1,) * value.ndim)
    return value + (corner * 0).astype(value.dtype)


def moved_to_head(own):
    heads = Y_HI * X
    pairs = []
    for y in range(Y_HI):
        for x in range(X):
            for p in range(Y_HI):
                for q in range(X):
                    for low in range(2):
                        for core in range(CORES):
                            source = (y * Z + 2 * x + low) * CORES + core
                            target = (p * Z + (2 * (x + q) + low) % Z) * CORES + core
                            pairs.append((source * heads + p * X + q, target * heads + y * X + x))
    return lax.ppermute(own, ("seq", "head"), pairs)


def gathered_rows(moved):
    columns = moved.shape[1]
    return lax.all_gather(moved, "seq", axis=0, tiled=True).reshape(Y_HI * X, -1, columns)


def head_product(weight, own):
    head = lax.axis_index("head")
    y, x = head // X, head % X

    def send(value, pairs):
        return lax.ppermute(value, "head", pairs)

    def term(value, flip, steps):
        block = lax.dynamic_index_in_dim(
            weight, (y ^ flip) * X + jnp.mod(2 * x - steps, X), 0, keepdims=False
        )
        return lax.dot_general(
            block, value, (((1,), (1,)), ((), ())), preferred_element_type=jnp.float32
        )

    half = own.shape[0] // 2
    below, above, across = send(own, X_UP), send(own, X_DOWN), send(own, Y_HI_SWAP)
    far = jnp.concatenate([send(below[:half], X_UP), send(above[half:], X_DOWN)])
    across_below, across_above = send(across, X_UP), send(across, X_DOWN)
    across_far = send(far, Y_HI_SWAP)
    total = term(own, 0, 0)
    for value, flip, steps in (
        (below, 0, 1),
        (above, 0, -1),
        (across, 1, 0),
        (far, 0, 2),
        (across_below, 1, 1),
        (across_above, 1, -1),
        (across_far, 1, 2),
    ):
        total = total + term(value, flip, steps)
    return total


def along(value, steps):
    count = lax.axis_size("seq")
    first, last = max(0, -steps), min(count, count - steps)
    return lax.ppermute(value, "seq", [(i, i + steps) for i in range(first, last)])


def gathered_weights(own, before):
    rows, columns = own.shape
    seq = lax.axis_index("seq")
    y, z, core = seq // (Z * CORES), (seq // CORES) % Z, seq % CORES
    other = lax.ppermute(own, "seq", Y_SWAP)
    low = jnp.where(y == 0, own, other)
    high = jnp.where(y == 0, other, own)
    pair = after(jnp.stack([low, high]), before)
    full = jnp.zeros((Y_LO, Z, CORES, rows, columns), own.dtype)

    def put(full, blocks):
        offsets = list(blocks)
        swapped = lax.ppermute(jnp.concatenate(list(blocks.values())), "seq", CORE_SWAP)
        for n, offset in enumerate(offsets):
            at = jnp.mod(z + offset, Z)
            for piece, c in ((blocks[offset], core), (swapped[2 * n : 2 * n + 2], 1 - core)):
                full = lax.dynamic_update_slice(full, piece[:, None, None], (0, at, c, 0, 0))
        return full

    up = down = pair
    full = put(full, {0: pair})
    for k in range(1, Z // 2):
        up = lax.ppermute(up, "seq", Z_UP)
        down = lax.ppermute(down, "seq", Z_DOWN)
        full = put(full, {-k: up, k: down})
    last = jnp.stack(
        [lax.ppermute(up[0], "seq", Z_UP), lax.ppermute(down[1], "seq", Z_DOWN)]
    )
    full = put(full, {Z // 2: last})
    return full.reshape(Y_LO * Z * CORES * rows, columns)


TILE = 128


def dot(a, b, contract):
    return lax.dot_general(a, b, ((contract[:1], contract[1:]), ((), ())), preferred_element_type=jnp.float32)


def unit_of(rows):
    rows = rows.astype(jnp.float32)
    inverse = lax.rsqrt(jnp.mean(rows * rows, axis=-1, keepdims=True) + norm_eps)
    return rows * inverse, inverse


def fill_window(second, first, own, keys, values):
    tokens = own.shape[1]
    for n, part in enumerate((second, first, own)):
        keys[n * tokens : (n + 1) * tokens, :] = part[0]
        values[n * tokens : (n + 1) * tokens, :] = part[1]


def forward_kernel(
    seq_ref, q_ref, second, first, own, readout_ref,
    raised_ref, inverse_ref, attended_ref, terms_ref, keys, values, query, total,
):
    tokens, reach = q_ref.shape[0], WINDOW_KEYS + TILE
    fill_window(second, first, own, keys, values)
    for g in range(2):
        unit, _ = unit_of(q_ref[:, g * HEAD_SIZE : (g + 1) * HEAD_SIZE])
        query[g] = (unit * (score_scale * LOG2_E)).astype(jnp.bfloat16)
    oldest = tokens * jnp.maximum(2 - seq_ref[0], 0)
    row = lax.broadcasted_iota(jnp.int32, (2 * TILE, TILE), 0) % TILE
    column = lax.broadcasted_iota(jnp.int32, (2 * TILE, TILE), 1)
    newer = (column > row).astype(jnp.float32)
    older = (column <= row).astype(jnp.float32)

    def tile(t, _):
        at = pl.multiple_of(t * TILE, TILE)
        window = pl.ds(at, reach)
        rows = pl.ds(at, TILE)
        both = jnp.concatenate([query[0, rows, :], query[1, rows, :]], axis=0)
        place = at + lax.broadcasted_iota(jnp.int32, (1, reach), 1)
        seen = (place >= oldest).astype(jnp.float32)
        raised = jnp.exp2(dot(both, keys[window, :], (1, 1))) * seen
        raised = jnp.concatenate(
            [raised[:, :TILE] * newer, raised[:, TILE:-TILE], raised[:, -TILE:] * older], axis=1
        )
        inverse = 1.0 / jnp.sum(raised, axis=-1, keepdims=True)
        kept = raised.astype(jnp.bfloat16)
        attended = (dot(kept, values[window, :], (1, 0)) * inverse).astype(jnp.bfloat16)
        for g in range(2):
            raised_ref[g, rows, :] = kept[g * TILE : (g + 1) * TILE]
            inverse_ref[g, rows, :] = inverse[g * TILE : (g + 1) * TILE]
            attended_ref[rows, g * HEAD_SIZE : (g + 1) * HEAD_SIZE] = attended[
                g * TILE : (g + 1) * TILE
            ]
        return 0

    lax.fori_loop(0, tokens // TILE, tile, 0)
    term = dot(attended_ref[...], readout_ref[...], (1, 0))

    @pl.when(pl.program_id(0) == 0)
    def _():
        total[...] = term

    @pl.when(pl.program_id(0) == 1)
    def _():
        terms_ref[...] = (total[...] + term).astype(jnp.bfloat16)


def backward_kernel(
    dlogits_ref, readout_ref, q_ref, raised_ref, inverse_ref, attended_ref, second, first, own,
    q_grad_ref, to_second, to_first, to_own,
    keys, values, query, upstream, key_sum, value_sum,
):
    tokens, reach = q_ref.shape[0], WINDOW_KEYS + TILE
    fill_window(second, first, own, keys, values)
    for g in range(2):
        unit, _ = unit_of(q_ref[:, g * HEAD_SIZE : (g + 1) * HEAD_SIZE])
        query[g] = unit.astype(jnp.bfloat16)
    upstream[...] = dot(dlogits_ref[...], readout_ref[...], (1, 1))
    key_sum[...] = jnp.zeros_like(key_sum)
    value_sum[...] = jnp.zeros_like(value_sum)

    def tile(t, _):
        at = pl.multiple_of(t * TILE, TILE)
        window = pl.ds(at, reach)
        rows = pl.ds(at, TILE)
        scaled, offset = [], []
        for g in range(2):
            columns = slice(g * HEAD_SIZE, (g + 1) * HEAD_SIZE)
            grad = upstream[rows, columns] * inverse_ref[g, rows, :]
            offset.append(
                jnp.sum(grad * attended_ref[rows, columns].astype(jnp.float32), axis=-1, keepdims=True)
            )
            scaled.append(grad.astype(jnp.bfloat16))
        scaled = jnp.concatenate(scaled, axis=0)
        offset = jnp.concatenate(offset, axis=0)
        raised = jnp.concatenate([raised_ref[0, rows, :], raised_ref[1, rows, :]], axis=0)
        both = jnp.concatenate([query[0, rows, :], query[1, rows, :]], axis=0)
        weights = dot(scaled, values[window, :], (1, 1))
        scores = (raised.astype(jnp.float32) * (weights - offset)).astype(jnp.bfloat16)
        value_sum[window, :] += dot(raised, scaled, (0, 0))
        key_sum[window, :] += dot(scores, both, (0, 0))
        hat = dot(scores, keys[window, :], (1, 0)) * score_scale
        for g in range(2):
            columns = slice(g * HEAD_SIZE, (g + 1) * HEAD_SIZE)
            unit, inverse = unit_of(q_ref[rows, columns])
            part = hat[g * TILE : (g + 1) * TILE]
            q_grad_ref[rows, columns] = inverse * (
                part - unit * jnp.mean(unit * part, axis=-1, keepdims=True)
            )
        return 0

    lax.fori_loop(0, tokens // TILE, tile, 0)
    for n, out in enumerate((to_second, to_first, to_own)):
        part = slice(n * tokens, (n + 1) * tokens)
        out[0] = (key_sum[part, :] * score_scale).astype(out.dtype)
        out[1] = value_sum[part, :].astype(out.dtype)


def normalize_kernel(projected_ref, out):
    width = out.shape[2]
    for low in range(0, width, HEAD_SIZE):
        columns = slice(low, low + HEAD_SIZE)
        out[0, :, columns] = unit_of(projected_ref[:, columns])[0].astype(jnp.bfloat16)
    out[1] = projected_ref[:, width:].astype(jnp.bfloat16)


def normalized(projected):
    tokens, width = projected.shape
    return pl.pallas_call(
        normalize_kernel,
        out_shape=jax.ShapeDtypeStruct((2, tokens, width // 2), jnp.bfloat16),
        cost_estimate=pl.CostEstimate(
            flops=2_000_000, bytes_accessed=1_500_000, transcendentals=1024
        ),
        name="normalized",
    )(projected)


def gradients_kernel(seq_ref, projected_ref, own, crossed, arrived, out):
    width = own.shape[2]
    keep = 1.0 - (seq_ref[0] % CORES).astype(jnp.float32)
    for low in range(0, width, HEAD_SIZE):
        columns = slice(low, low + HEAD_SIZE)
        unit, inverse = unit_of(projected_ref[:, columns])
        keys, values = (
            own[n, :, columns]
            + arrived[n, :, columns].astype(jnp.float32)
            + keep * crossed[n, :, columns].astype(jnp.float32)
            for n in range(2)
        )
        keys = inverse * (keys - unit * jnp.mean(unit * keys, axis=-1, keepdims=True))
        out[:, columns] = keys.astype(jnp.bfloat16)
        out[:, width + low : width + low + HEAD_SIZE] = values.astype(jnp.bfloat16)


def projection_gradients(seq, projected, own, crossed, arrived):
    vmem = pl.BlockSpec(memory_space=pltpu.VMEM)
    return pl.pallas_call(
        gradients_kernel,
        in_specs=[pl.BlockSpec(memory_space=pltpu.SMEM), vmem, vmem, vmem, vmem],
        out_specs=vmem,
        out_shape=jax.ShapeDtypeStruct(projected.shape, jnp.bfloat16),
        cost_estimate=pl.CostEstimate(
            flops=4_000_000, bytes_accessed=3_500_000, transcendentals=1024
        ),
        name="projection_gradients",
    )(seq.reshape(1), projected, own, crossed, arrived)


def window_specs(tokens):
    return [pl.BlockSpec((2, tokens, HEAD_SIZE), lambda k: (0, 0, k))] * 3


def attention_forward(seq, queries, second, first, own, readout):
    tokens, width = queries.shape
    kv_heads, reach = own.shape[2] // HEAD_SIZE, WINDOW_KEYS + TILE
    candidates = readout.shape[1]
    return pl.pallas_call(
        forward_kernel,
        grid=(kv_heads,),
        in_specs=[
            pl.BlockSpec(memory_space=pltpu.SMEM),
            pl.BlockSpec((tokens, 2 * HEAD_SIZE), lambda k: (0, k)),
            *window_specs(tokens),
            pl.BlockSpec((2 * HEAD_SIZE, candidates), lambda k: (k, 0)),
        ],
        out_specs=[
            pl.BlockSpec((2, tokens, reach), lambda k: (k, 0, 0)),
            pl.BlockSpec((2, tokens, 1), lambda k: (k, 0, 0)),
            pl.BlockSpec((tokens, 2 * HEAD_SIZE), lambda k: (0, k)),
            pl.BlockSpec((tokens, candidates), lambda k: (0, 0)),
        ],
        out_shape=[
            jax.ShapeDtypeStruct((2 * kv_heads, tokens, reach), jnp.bfloat16),
            jax.ShapeDtypeStruct((2 * kv_heads, tokens, 1), jnp.float32),
            jax.ShapeDtypeStruct((tokens, width), jnp.bfloat16),
            jax.ShapeDtypeStruct((tokens, candidates), jnp.bfloat16),
        ],
        scratch_shapes=[
            pltpu.VMEM((3 * tokens, HEAD_SIZE), jnp.bfloat16),
            pltpu.VMEM((3 * tokens, HEAD_SIZE), jnp.bfloat16),
            pltpu.VMEM((2, tokens, HEAD_SIZE), jnp.bfloat16),
            pltpu.VMEM((tokens, candidates), jnp.float32),
        ],
        compiler_params=pltpu.CompilerParams(dimension_semantics=("arbitrary",)),
        cost_estimate=pl.CostEstimate(
            flops=2_500_000_000, bytes_accessed=8_000_000, transcendentals=2_400_000
        ),
        name="attention_forward",
    )(seq.reshape(1), queries, second, first, own, readout)


def attention_backward(dlogits, readout, queries, raised, inverse, attended, second, first, own):
    tokens, width = queries.shape
    kv_heads, reach = own.shape[2] // HEAD_SIZE, WINDOW_KEYS + TILE
    candidates = readout.shape[1]
    pair = pl.BlockSpec((tokens, 2 * HEAD_SIZE), lambda k: (0, k))
    return pl.pallas_call(
        backward_kernel,
        grid=(kv_heads,),
        in_specs=[
            pl.BlockSpec((tokens, candidates), lambda k: (0, 0)),
            pl.BlockSpec((2 * HEAD_SIZE, candidates), lambda k: (k, 0)),
            pair,
            pl.BlockSpec((2, tokens, reach), lambda k: (k, 0, 0)),
            pl.BlockSpec((2, tokens, 1), lambda k: (k, 0, 0)),
            pair,
            *window_specs(tokens),
        ],
        out_specs=[pair, *window_specs(tokens)],
        out_shape=[
            jax.ShapeDtypeStruct((tokens, width), jnp.float32),
            jax.ShapeDtypeStruct(own.shape, jnp.bfloat16),
            jax.ShapeDtypeStruct(own.shape, jnp.bfloat16),
            jax.ShapeDtypeStruct(own.shape, jnp.float32),
        ],
        scratch_shapes=[
            pltpu.VMEM((3 * tokens, HEAD_SIZE), jnp.bfloat16),
            pltpu.VMEM((3 * tokens, HEAD_SIZE), jnp.bfloat16),
            pltpu.VMEM((2, tokens, HEAD_SIZE), jnp.bfloat16),
            pltpu.VMEM((tokens, 2 * HEAD_SIZE), jnp.float32),
            pltpu.VMEM((3 * tokens, HEAD_SIZE), jnp.float32),
            pltpu.VMEM((3 * tokens, HEAD_SIZE), jnp.float32),
        ],
        compiler_params=pltpu.CompilerParams(dimension_semantics=("arbitrary",)),
        cost_estimate=pl.CostEstimate(
            flops=5_000_000_000, bytes_accessed=12_000_000, transcendentals=0
        ),
        name="attention_backward",
    )(dlogits, readout, queries, raised, inverse, attended, second, first, own)


def shards(inputs, queries, key_matrix, value_matrix, readout, token_mask, targets):
    tokens = inputs.shape[0]
    heads = lax.axis_size("head")
    seq = lax.axis_index("seq")
    core = seq % CORES
    own_weight = jnp.concatenate([key_matrix, value_matrix], axis=1)
    moved = moved_to_head(own_weight)
    full_weight = gathered_weights(own_weight, moved)
    projected = jnp.dot(inputs, full_weight, preferred_element_type=jnp.float32)
    paired = normalized(projected)
    second = along(paired, 2)
    first = lax.ppermute(jnp.where(core == 0, paired, second), "seq", CORE_SWAP)
    rows_weight = gathered_rows(after(moved, second))
    raised, inverse, attended, partial_value = attention_forward(
        seq, queries, second, first, paired, readout
    )


    share = tokens // heads
    terms = lax.all_to_all(partial_value, "head", 0, 0, tiled=True)
    logits = jnp.sum(terms.astype(jnp.float32).reshape(heads, share, -1), axis=0)
    mine = lax.axis_index("head") * share
    wanted = lax.dynamic_slice_in_dim(targets, mine, share, 0)
    chosen = lax.dynamic_slice_in_dim(token_mask, mine, share, 0).astype(jnp.float32)[:, None]
    capped = softcap * jnp.tanh(logits / softcap)
    expo = jnp.exp(capped)
    probs = expo / jnp.sum(expo, axis=-1, keepdims=True)
    onehot = (wanted[:, None] == jnp.arange(logits.shape[1], dtype=jnp.int32)[None, :]).astype(
        jnp.float32
    )
    dlogits = (chosen * (probs - onehot) * (1.0 - (capped / softcap) ** 2)).astype(jnp.bfloat16)
    dlogits = lax.all_to_all(
        jnp.broadcast_to(dlogits[None], (heads,) + dlogits.shape), "head", 0, 0, tiled=True
    ).reshape(tokens, -1)

    query_grad, to_second, to_first, total = attention_backward(
        dlogits, readout, queries, raised, inverse, attended, second, first, paired
    )
    crossed = lax.ppermute(to_first, "seq", CORE_SWAP)
    outgoing = to_second.astype(jnp.float32) + jnp.where(core == 1, crossed, 0).astype(jnp.float32)
    arrived = along(outgoing.astype(jnp.bfloat16), -2)
    both_grad = projection_gradients(seq, projected, total, crossed, arrived)
    input_grad = head_product(rows_weight, both_grad).T
    return (query_grad, input_grad)


def solution(mesh):
    in_specs = (
        P("seq", None),
        P("seq", "head"),
        P("seq", "head"),
        P("seq", "head"),
        P("head", None),
        P("seq"),
        P("seq"),
    )
    out_specs = (P("seq", "head"), P("seq", "head"))
    return jax.shard_map(shards, mesh=mesh, in_specs=in_specs, out_specs=out_specs, check_vma=False)
```

```python
import jax
import jax.numpy as jnp
from jax import lax
from jax.experimental import pallas as pl
from jax.experimental.pallas import tpu as pltpu
from jax.sharding import PartitionSpec as P

HEAD_SIZE = 128
WINDOW_KEYS = 1024

norm_eps = 1e-06
softcap = 30.0
score_scale = 168.0 ** (-0.5)
LOG2_E = 1.4426950408889634

Y_LO, Z, CORES = 2, 8, 2
Y_HI, X = 2, 4


def seq_pairs(move):
    pairs = []
    for y in range(Y_LO):
        for z in range(Z):
            for c in range(CORES):
                ty, tz, tc = move(y, z, c)
                pairs.append(((y * Z + z) * CORES + c, (ty * Z + tz) * CORES + tc))
    return pairs


CORE_SWAP = seq_pairs(lambda y, z, c: (y, z, 1 - c))
Y_SWAP = seq_pairs(lambda y, z, c: (1 - y, z, c))
Z_UP = seq_pairs(lambda y, z, c: (y, (z + 1) % Z, c))
Z_DOWN = seq_pairs(lambda y, z, c: (y, (z - 1) % Z, c))


def head_pairs(flip, steps):
    return [
        (y * X + x, (y ^ flip) * X + (x + steps) % X) for y in range(Y_HI) for x in range(X)
    ]


X_UP, X_DOWN, Y_HI_SWAP = head_pairs(0, 1), head_pairs(0, -1), head_pairs(1, 0)


def after(value, other):
    corner = other[(slice(0, 1),) * other.ndim].reshape((1,) * value.ndim)
    return value + (corner * 0).astype(value.dtype)


def moved_to_head(own):
    heads = Y_HI * X
    pairs = []
    for y in range(Y_HI):
        for x in range(X):
            for p in range(Y_HI):
                for q in range(X):
                    for low in range(2):
                        for core in range(CORES):
                            source = (y * Z + 2 * x + low) * CORES + core
                            target = (p * Z + (2 * (x + q) + low) % Z) * CORES + core
                            pairs.append((source * heads + p * X + q, target * heads + y * X + x))
    return lax.ppermute(own, ("seq", "head"), pairs)


def gathered_rows(moved):
    columns = moved.shape[1]
    return lax.all_gather(moved, "seq", axis=0, tiled=True).reshape(Y_HI * X, -1, columns)


def head_product(weight, own):
    head = lax.axis_index("head")
    y, x = head // X, head % X

    def send(value, pairs):
        return lax.ppermute(value, "head", pairs)

    def term(value, flip, steps):
        block = lax.dynamic_index_in_dim(
            weight, (y ^ flip) * X + jnp.mod(2 * x - steps, X), 0, keepdims=False
        )
        return lax.dot_general(
            block, value, (((1,), (1,)), ((), ())), preferred_element_type=jnp.float32
        )

    half = own.shape[0] // 2
    below, above, across = send(own, X_UP), send(own, X_DOWN), send(own, Y_HI_SWAP)
    far = jnp.concatenate([send(below[:half], X_UP), send(above[half:], X_DOWN)])
    across_below, across_above = send(across, X_UP), send(across, X_DOWN)
    across_far = send(far, Y_HI_SWAP)
    total = term(own, 0, 0)
    for value, flip, steps in (
        (below, 0, 1),
        (above, 0, -1),
        (across, 1, 0),
        (far, 0, 2),
        (across_below, 1, 1),
        (across_above, 1, -1),
        (across_far, 1, 2),
    ):
        total = total + term(value, flip, steps)
    return total


def along(value, steps):
    count = lax.axis_size("seq")
    first, last = max(0, -steps), min(count, count - steps)
    return lax.ppermute(value, "seq", [(i, i + steps) for i in range(first, last)])


def gathered_weights(own, before):
    rows, columns = own.shape
    seq = lax.axis_index("seq")
    y, z, core = seq // (Z * CORES), (seq // CORES) % Z, seq % CORES
    other = lax.ppermute(own, "seq", Y_SWAP)
    low = jnp.where(y == 0, own, other)
    high = jnp.where(y == 0, other, own)
    pair = after(jnp.stack([low, high]), before)
    full = jnp.zeros((Y_LO, Z, CORES, rows, columns), own.dtype)

    def put(full, blocks):
        offsets = list(blocks)
        swapped = lax.ppermute(jnp.concatenate(list(blocks.values())), "seq", CORE_SWAP)
        for n, offset in enumerate(offsets):
            at = jnp.mod(z + offset, Z)
            for piece, c in ((blocks[offset], core), (swapped[2 * n : 2 * n + 2], 1 - core)):
                full = lax.dynamic_update_slice(full, piece[:, None, None], (0, at, c, 0, 0))
        return full

    up = down = pair
    full = put(full, {0: pair})
    for k in range(1, Z // 2):
        up = lax.ppermute(up, "seq", Z_UP)
        down = lax.ppermute(down, "seq", Z_DOWN)
        full = put(full, {-k: up, k: down})
    last = jnp.stack(
        [lax.ppermute(up[0], "seq", Z_UP), lax.ppermute(down[1], "seq", Z_DOWN)]
    )
    full = put(full, {Z // 2: last})
    return full.reshape(Y_LO * Z * CORES * rows, columns)


TILE = 128
ATTENTION_VMEM = 50 << 20
SMALL_VMEM = 16 << 20


def dot(a, b, contract):
    return lax.dot_general(a, b, ((contract[:1], contract[1:]), ((), ())), preferred_element_type=jnp.float32)


def unit_of(rows):
    rows = rows.astype(jnp.float32)
    inverse = lax.rsqrt(jnp.mean(rows * rows, axis=-1, keepdims=True) + norm_eps)
    return rows * inverse, inverse


def fill_window(second, first, own, keys, values):
    tokens = own.shape[1]
    for n, part in enumerate((second, first, own)):
        keys[n * tokens : (n + 1) * tokens, :] = part[0]
        values[n * tokens : (n + 1) * tokens, :] = part[1]


def forward_kernel(
    seq_ref, q_ref, second, first, own, readout_ref,
    raised_ref, inverse_ref, attended_ref, terms_ref, keys, values, query, total,
):
    tokens, reach = q_ref.shape[0], WINDOW_KEYS + TILE
    fill_window(second, first, own, keys, values)
    for g in range(2):
        unit, _ = unit_of(q_ref[:, g * HEAD_SIZE : (g + 1) * HEAD_SIZE])
        query[g] = (unit * (score_scale * LOG2_E)).astype(jnp.bfloat16)
    oldest = tokens * jnp.maximum(2 - seq_ref[0], 0)
    row = lax.broadcasted_iota(jnp.int32, (2 * TILE, TILE), 0) % TILE
    column = lax.broadcasted_iota(jnp.int32, (2 * TILE, TILE), 1)
    newer = (column > row).astype(jnp.float32)
    older = (column <= row).astype(jnp.float32)

    def tile(t, _):
        at = pl.multiple_of(t * TILE, TILE)
        window = pl.ds(at, reach)
        rows = pl.ds(at, TILE)
        both = jnp.concatenate([query[0, rows, :], query[1, rows, :]], axis=0)
        place = at + lax.broadcasted_iota(jnp.int32, (1, reach), 1)
        seen = (place >= oldest).astype(jnp.float32)
        raised = jnp.exp2(dot(both, keys[window, :], (1, 1))) * seen
        raised = jnp.concatenate(
            [raised[:, :TILE] * newer, raised[:, TILE:-TILE], raised[:, -TILE:] * older], axis=1
        )
        inverse = 1.0 / jnp.sum(raised, axis=-1, keepdims=True)
        kept = raised.astype(jnp.bfloat16)
        attended = (dot(kept, values[window, :], (1, 0)) * inverse).astype(jnp.bfloat16)
        for g in range(2):
            raised_ref[g, rows, :] = kept[g * TILE : (g + 1) * TILE]
            inverse_ref[g, rows, :] = inverse[g * TILE : (g + 1) * TILE]
            attended_ref[rows, g * HEAD_SIZE : (g + 1) * HEAD_SIZE] = attended[
                g * TILE : (g + 1) * TILE
            ]
        return 0

    lax.fori_loop(0, tokens // TILE, tile, 0)
    term = dot(attended_ref[...], readout_ref[...], (1, 0))

    @pl.when(pl.program_id(0) == 0)
    def _():
        total[...] = term

    @pl.when(pl.program_id(0) == 1)
    def _():
        terms_ref[...] = (total[...] + term).astype(jnp.bfloat16)


def backward_kernel(
    dlogits_ref, readout_ref, q_ref, raised_ref, inverse_ref, attended_ref, second, first, own,
    q_grad_ref, to_second, to_first, to_own,
    keys, values, query, upstream, key_sum, value_sum,
):
    tokens, reach = q_ref.shape[0], WINDOW_KEYS + TILE
    fill_window(second, first, own, keys, values)
    for g in range(2):
        unit, _ = unit_of(q_ref[:, g * HEAD_SIZE : (g + 1) * HEAD_SIZE])
        query[g] = unit.astype(jnp.bfloat16)
    upstream[...] = dot(dlogits_ref[...], readout_ref[...], (1, 1))
    key_sum[...] = jnp.zeros_like(key_sum)
    value_sum[...] = jnp.zeros_like(value_sum)

    def tile(t, _):
        at = pl.multiple_of(t * TILE, TILE)
        window = pl.ds(at, reach)
        rows = pl.ds(at, TILE)
        scaled, offset = [], []
        for g in range(2):
            columns = slice(g * HEAD_SIZE, (g + 1) * HEAD_SIZE)
            grad = upstream[rows, columns] * inverse_ref[g, rows, :]
            offset.append(
                jnp.sum(grad * attended_ref[rows, columns].astype(jnp.float32), axis=-1, keepdims=True)
            )
            scaled.append(grad.astype(jnp.bfloat16))
        scaled = jnp.concatenate(scaled, axis=0)
        offset = jnp.concatenate(offset, axis=0)
        raised = jnp.concatenate([raised_ref[0, rows, :], raised_ref[1, rows, :]], axis=0)
        both = jnp.concatenate([query[0, rows, :], query[1, rows, :]], axis=0)
        weights = dot(scaled, values[window, :], (1, 1))
        scores = (raised.astype(jnp.float32) * (weights - offset)).astype(jnp.bfloat16)
        value_sum[window, :] += dot(raised, scaled, (0, 0))
        key_sum[window, :] += dot(scores, both, (0, 0))
        hat = dot(scores, keys[window, :], (1, 0)) * score_scale
        for g in range(2):
            columns = slice(g * HEAD_SIZE, (g + 1) * HEAD_SIZE)
            unit, inverse = unit_of(q_ref[rows, columns])
            part = hat[g * TILE : (g + 1) * TILE]
            q_grad_ref[rows, columns] = inverse * (
                part - unit * jnp.mean(unit * part, axis=-1, keepdims=True)
            )
        return 0

    lax.fori_loop(0, tokens // TILE, tile, 0)
    for n, out in enumerate((to_second, to_first, to_own)):
        part = slice(n * tokens, (n + 1) * tokens)
        out[0] = (key_sum[part, :] * score_scale).astype(out.dtype)
        out[1] = value_sum[part, :].astype(out.dtype)


def normalize_kernel(projected_ref, out):
    width = out.shape[2]
    for low in range(0, width, HEAD_SIZE):
        columns = slice(low, low + HEAD_SIZE)
        out[0, :, columns] = unit_of(projected_ref[:, columns])[0].astype(jnp.bfloat16)
    out[1] = projected_ref[:, width:].astype(jnp.bfloat16)


def normalized(projected):
    tokens, width = projected.shape
    return pl.pallas_call(
        normalize_kernel,
        out_shape=jax.ShapeDtypeStruct((2, tokens, width // 2), jnp.bfloat16),
        cost_estimate=pl.CostEstimate(
            flops=2_000_000, bytes_accessed=1_500_000, transcendentals=1024
        ),
        compiler_params=pltpu.CompilerParams(vmem_limit_bytes=SMALL_VMEM),
        name="normalized",
    )(projected)


def gradients_kernel(seq_ref, projected_ref, own, crossed, arrived, out):
    width = own.shape[2]
    keep = 1.0 - (seq_ref[0] % CORES).astype(jnp.float32)
    for low in range(0, width, HEAD_SIZE):
        columns = slice(low, low + HEAD_SIZE)
        unit, inverse = unit_of(projected_ref[:, columns])
        keys, values = (
            own[n, :, columns]
            + arrived[n, :, columns].astype(jnp.float32)
            + keep * crossed[n, :, columns].astype(jnp.float32)
            for n in range(2)
        )
        keys = inverse * (keys - unit * jnp.mean(unit * keys, axis=-1, keepdims=True))
        out[:, columns] = keys.astype(jnp.bfloat16)
        out[:, width + low : width + low + HEAD_SIZE] = values.astype(jnp.bfloat16)


def projection_gradients(seq, projected, own, crossed, arrived):
    vmem = pl.BlockSpec(memory_space=pltpu.VMEM)
    return pl.pallas_call(
        gradients_kernel,
        in_specs=[pl.BlockSpec(memory_space=pltpu.SMEM), vmem, vmem, vmem, vmem],
        out_specs=vmem,
        out_shape=jax.ShapeDtypeStruct(projected.shape, jnp.bfloat16),
        cost_estimate=pl.CostEstimate(
            flops=4_000_000, bytes_accessed=3_500_000, transcendentals=1024
        ),
        compiler_params=pltpu.CompilerParams(vmem_limit_bytes=SMALL_VMEM),
        name="projection_gradients",
    )(seq.reshape(1), projected, own, crossed, arrived)


def window_specs(tokens):
    return [pl.BlockSpec((2, tokens, HEAD_SIZE), lambda k: (0, 0, k))] * 3


def attention_forward(seq, queries, second, first, own, readout):
    tokens, width = queries.shape
    kv_heads, reach = own.shape[2] // HEAD_SIZE, WINDOW_KEYS + TILE
    candidates = readout.shape[1]
    return pl.pallas_call(
        forward_kernel,
        grid=(kv_heads,),
        in_specs=[
            pl.BlockSpec(memory_space=pltpu.SMEM),
            pl.BlockSpec((tokens, 2 * HEAD_SIZE), lambda k: (0, k)),
            *window_specs(tokens),
            pl.BlockSpec((2 * HEAD_SIZE, candidates), lambda k: (k, 0)),
        ],
        out_specs=[
            pl.BlockSpec((2, tokens, reach), lambda k: (k, 0, 0)),
            pl.BlockSpec((2, tokens, 1), lambda k: (k, 0, 0)),
            pl.BlockSpec((tokens, 2 * HEAD_SIZE), lambda k: (0, k)),
            pl.BlockSpec((tokens, candidates), lambda k: (0, 0)),
        ],
        out_shape=[
            jax.ShapeDtypeStruct((2 * kv_heads, tokens, reach), jnp.bfloat16),
            jax.ShapeDtypeStruct((2 * kv_heads, tokens, 1), jnp.float32),
            jax.ShapeDtypeStruct((tokens, width), jnp.bfloat16),
            jax.ShapeDtypeStruct((tokens, candidates), jnp.bfloat16),
        ],
        scratch_shapes=[
            pltpu.VMEM((3 * tokens, HEAD_SIZE), jnp.bfloat16),
            pltpu.VMEM((3 * tokens, HEAD_SIZE), jnp.bfloat16),
            pltpu.VMEM((2, tokens, HEAD_SIZE), jnp.bfloat16),
            pltpu.VMEM((tokens, candidates), jnp.float32),
        ],
        compiler_params=pltpu.CompilerParams(
            dimension_semantics=("arbitrary",), vmem_limit_bytes=ATTENTION_VMEM
        ),
        cost_estimate=pl.CostEstimate(
            flops=2_500_000_000, bytes_accessed=8_000_000, transcendentals=2_400_000
        ),
        name="attention_forward",
    )(seq.reshape(1), queries, second, first, own, readout)


def attention_backward(dlogits, readout, queries, raised, inverse, attended, second, first, own):
    tokens, width = queries.shape
    kv_heads, reach = own.shape[2] // HEAD_SIZE, WINDOW_KEYS + TILE
    candidates = readout.shape[1]
    pair = pl.BlockSpec((tokens, 2 * HEAD_SIZE), lambda k: (0, k))
    return pl.pallas_call(
        backward_kernel,
        grid=(kv_heads,),
        in_specs=[
            pl.BlockSpec((tokens, candidates), lambda k: (0, 0)),
            pl.BlockSpec((2 * HEAD_SIZE, candidates), lambda k: (k, 0)),
            pair,
            pl.BlockSpec((2, tokens, reach), lambda k: (k, 0, 0)),
            pl.BlockSpec((2, tokens, 1), lambda k: (k, 0, 0)),
            pair,
            *window_specs(tokens),
        ],
        out_specs=[pair, *window_specs(tokens)],
        out_shape=[
            jax.ShapeDtypeStruct((tokens, width), jnp.float32),
            jax.ShapeDtypeStruct(own.shape, jnp.bfloat16),
            jax.ShapeDtypeStruct(own.shape, jnp.bfloat16),
            jax.ShapeDtypeStruct(own.shape, jnp.float32),
        ],
        scratch_shapes=[
            pltpu.VMEM((3 * tokens, HEAD_SIZE), jnp.bfloat16),
            pltpu.VMEM((3 * tokens, HEAD_SIZE), jnp.bfloat16),
            pltpu.VMEM((2, tokens, HEAD_SIZE), jnp.bfloat16),
            pltpu.VMEM((tokens, 2 * HEAD_SIZE), jnp.float32),
            pltpu.VMEM((3 * tokens, HEAD_SIZE), jnp.float32),
            pltpu.VMEM((3 * tokens, HEAD_SIZE), jnp.float32),
        ],
        compiler_params=pltpu.CompilerParams(
            dimension_semantics=("arbitrary",), vmem_limit_bytes=ATTENTION_VMEM
        ),
        cost_estimate=pl.CostEstimate(
            flops=5_000_000_000, bytes_accessed=12_000_000, transcendentals=0
        ),
        name="attention_backward",
    )(dlogits, readout, queries, raised, inverse, attended, second, first, own)


def shards(inputs, queries, key_matrix, value_matrix, readout, token_mask, targets):
    tokens = inputs.shape[0]
    heads = lax.axis_size("head")
    seq = lax.axis_index("seq")
    core = seq % CORES
    own_weight = jnp.concatenate([key_matrix, value_matrix], axis=1)
    moved = moved_to_head(own_weight)
    full_weight = gathered_weights(own_weight, moved)
    projected = jnp.dot(inputs, full_weight, preferred_element_type=jnp.float32)
    paired = normalized(projected)
    second = along(paired, 2)
    first = lax.ppermute(jnp.where(core == 0, paired, second), "seq", CORE_SWAP)
    rows_weight = gathered_rows(after(moved, second))
    raised, inverse, attended, partial_value = attention_forward(
        seq, queries, second, first, paired, readout
    )


    share = tokens // heads
    terms = lax.all_to_all(partial_value, "head", 0, 0, tiled=True)
    logits = jnp.sum(terms.astype(jnp.float32).reshape(heads, share, -1), axis=0)
    mine = lax.axis_index("head") * share
    wanted = lax.dynamic_slice_in_dim(targets, mine, share, 0)
    chosen = lax.dynamic_slice_in_dim(token_mask, mine, share, 0).astype(jnp.float32)[:, None]
    capped = softcap * jnp.tanh(logits / softcap)
    expo = jnp.exp(capped)
    probs = expo / jnp.sum(expo, axis=-1, keepdims=True)
    onehot = (wanted[:, None] == jnp.arange(logits.shape[1], dtype=jnp.int32)[None, :]).astype(
        jnp.float32
    )
    dlogits = (chosen * (probs - onehot) * (1.0 - (capped / softcap) ** 2)).astype(jnp.bfloat16)
    dlogits = lax.all_to_all(
        jnp.broadcast_to(dlogits[None], (heads,) + dlogits.shape), "head", 0, 0, tiled=True
    ).reshape(tokens, -1)

    query_grad, to_second, to_first, total = attention_backward(
        dlogits, readout, queries, raised, inverse, attended, second, first, paired
    )
    crossed = lax.ppermute(to_first, "seq", CORE_SWAP)
    outgoing = to_second.astype(jnp.float32) + jnp.where(core == 1, crossed, 0).astype(jnp.float32)
    arrived = along(outgoing.astype(jnp.bfloat16), -2)
    both_grad = projection_gradients(seq, projected, total, crossed, arrived)
    input_grad = head_product(rows_weight, both_grad).T
    return (query_grad, input_grad)


def solution(mesh):
    in_specs = (
        P("seq", None),
        P("seq", "head"),
        P("seq", "head"),
        P("seq", "head"),
        P("head", None),
        P("seq"),
        P("seq"),
    )
    out_specs = (P("seq", "head"), P("seq", "head"))
    return jax.shard_map(shards, mesh=mesh, in_specs=in_specs, out_specs=out_specs, check_vma=False)
```

```python
import jax
import jax.numpy as jnp
from jax import lax
from jax.experimental import pallas as pl
from jax.experimental.pallas import tpu as pltpu
from jax.sharding import PartitionSpec as P

HEAD_SIZE = 128
WINDOW_KEYS = 1024

norm_eps = 1e-06
softcap = 30.0
score_scale = 168.0 ** (-0.5)
LOG2_E = 1.4426950408889634

Y_LO, Z, CORES = 2, 8, 2
Y_HI, X = 2, 4


def seq_pairs(move):
    pairs = []
    for y in range(Y_LO):
        for z in range(Z):
            for c in range(CORES):
                ty, tz, tc = move(y, z, c)
                pairs.append(((y * Z + z) * CORES + c, (ty * Z + tz) * CORES + tc))
    return pairs


CORE_SWAP = seq_pairs(lambda y, z, c: (y, z, 1 - c))
Y_SWAP = seq_pairs(lambda y, z, c: (1 - y, z, c))
Z_UP = seq_pairs(lambda y, z, c: (y, (z + 1) % Z, c))
Z_DOWN = seq_pairs(lambda y, z, c: (y, (z - 1) % Z, c))


def head_pairs(flip, steps):
    return [
        (y * X + x, (y ^ flip) * X + (x + steps) % X) for y in range(Y_HI) for x in range(X)
    ]


X_UP, X_DOWN, Y_HI_SWAP = head_pairs(0, 1), head_pairs(0, -1), head_pairs(1, 0)


def after(value, other):
    corner = other[(slice(0, 1),) * other.ndim].reshape((1,) * value.ndim)
    return value + (corner * 0).astype(value.dtype)


def moved_to_head(own):
    heads = Y_HI * X
    pairs = []
    for y in range(Y_HI):
        for x in range(X):
            for p in range(Y_HI):
                for q in range(X):
                    for low in range(2):
                        for core in range(CORES):
                            source = (y * Z + 2 * x + low) * CORES + core
                            target = (p * Z + (2 * (x + q) + low) % Z) * CORES + core
                            pairs.append((source * heads + p * X + q, target * heads + y * X + x))
    return lax.ppermute(own, ("seq", "head"), pairs)


def gathered_rows(moved):
    columns = moved.shape[1]
    return lax.all_gather(moved, "seq", axis=0, tiled=True).reshape(Y_HI * X, -1, columns)


def head_product(weight, own):
    head = lax.axis_index("head")
    y, x = head // X, head % X

    def send(value, pairs):
        return lax.ppermute(value, "head", pairs)

    def term(value, flip, steps):
        block = lax.dynamic_index_in_dim(
            weight, (y ^ flip) * X + jnp.mod(2 * x - steps, X), 0, keepdims=False
        )
        return lax.dot_general(
            block, value, (((1,), (1,)), ((), ())), preferred_element_type=jnp.float32
        )

    half = own.shape[0] // 2
    below, above, across = send(own, X_UP), send(own, X_DOWN), send(own, Y_HI_SWAP)
    far = jnp.concatenate([send(below[:half], X_UP), send(above[half:], X_DOWN)])
    across_below, across_above = send(across, X_UP), send(across, X_DOWN)
    across_far = send(far, Y_HI_SWAP)
    total = term(own, 0, 0)
    for value, flip, steps in (
        (below, 0, 1),
        (above, 0, -1),
        (across, 1, 0),
        (far, 0, 2),
        (across_below, 1, 1),
        (across_above, 1, -1),
    ):
        total = total + term(value, flip, steps)
    return lax.optimization_barrier(total) + term(across_far, 1, 2)


def along(value, steps):
    count = lax.axis_size("seq")
    first, last = max(0, -steps), min(count, count - steps)
    return lax.ppermute(value, "seq", [(i, i + steps) for i in range(first, last)])


def gathered_weights(own):
    rows, columns = own.shape
    seq = lax.axis_index("seq")
    y, z, core = seq // (Z * CORES), (seq // CORES) % Z, seq % CORES
    other = lax.ppermute(own, "seq", Y_SWAP)
    low = jnp.where(y == 0, own, other)
    high = jnp.where(y == 0, other, own)
    pair = jnp.stack([low, high])
    full = jnp.zeros((Y_LO, Z, CORES, rows, columns), own.dtype)

    def put(full, blocks):
        offsets = list(blocks)
        swapped = lax.ppermute(jnp.concatenate(list(blocks.values())), "seq", CORE_SWAP)
        for n, offset in enumerate(offsets):
            at = jnp.mod(z + offset, Z)
            for piece, c in ((blocks[offset], core), (swapped[2 * n : 2 * n + 2], 1 - core)):
                full = lax.dynamic_update_slice(full, piece[:, None, None], (0, at, c, 0, 0))
        return full

    up = down = pair
    full = put(full, {0: pair})
    for k in range(1, Z // 2):
        up = lax.ppermute(up, "seq", Z_UP)
        down = lax.ppermute(down, "seq", Z_DOWN)
        full = put(full, {-k: up, k: down})
    last = jnp.stack(
        [lax.ppermute(up[0], "seq", Z_UP), lax.ppermute(down[1], "seq", Z_DOWN)]
    )
    full = put(full, {Z // 2: last})
    return full.reshape(Y_LO * Z * CORES * rows, columns)


TILE = 128
ATTENTION_VMEM = 50 << 20
SMALL_VMEM = 16 << 20


def dot(a, b, contract):
    return lax.dot_general(a, b, ((contract[:1], contract[1:]), ((), ())), preferred_element_type=jnp.float32)


def unit_of(rows):
    rows = rows.astype(jnp.float32)
    inverse = lax.rsqrt(jnp.mean(rows * rows, axis=-1, keepdims=True) + norm_eps)
    return rows * inverse, inverse


def fill_window(second, first, own, keys, values):
    tokens = own.shape[1]
    for n, part in enumerate((second, first, own)):
        keys[n * tokens : (n + 1) * tokens, :] = part[0]
        values[n * tokens : (n + 1) * tokens, :] = part[1]


def forward_kernel(
    seq_ref, q_ref, second, first, own, readout_ref,
    raised_ref, inverse_ref, attended_ref, terms_ref, keys, values, query, total,
):
    tokens, reach = q_ref.shape[0], WINDOW_KEYS + TILE
    fill_window(second, first, own, keys, values)
    for g in range(2):
        unit, _ = unit_of(q_ref[:, g * HEAD_SIZE : (g + 1) * HEAD_SIZE])
        query[g] = (unit * (score_scale * LOG2_E)).astype(jnp.bfloat16)
    oldest = tokens * jnp.maximum(2 - seq_ref[0], 0)
    row = lax.broadcasted_iota(jnp.int32, (2 * TILE, TILE), 0) % TILE
    column = lax.broadcasted_iota(jnp.int32, (2 * TILE, TILE), 1)
    newer = (column > row).astype(jnp.float32)
    older = (column <= row).astype(jnp.float32)

    def tile(t, _):
        at = pl.multiple_of(t * TILE, TILE)
        window = pl.ds(at, reach)
        rows = pl.ds(at, TILE)
        both = jnp.concatenate([query[0, rows, :], query[1, rows, :]], axis=0)
        place = at + lax.broadcasted_iota(jnp.int32, (1, reach), 1)
        seen = (place >= oldest).astype(jnp.float32)
        raised = jnp.exp2(dot(both, keys[window, :], (1, 1))) * seen
        raised = jnp.concatenate(
            [raised[:, :TILE] * newer, raised[:, TILE:-TILE], raised[:, -TILE:] * older], axis=1
        )
        inverse = 1.0 / jnp.sum(raised, axis=-1, keepdims=True)
        kept = raised.astype(jnp.bfloat16)
        attended = (dot(kept, values[window, :], (1, 0)) * inverse).astype(jnp.bfloat16)
        for g in range(2):
            raised_ref[g, rows, :] = kept[g * TILE : (g + 1) * TILE]
            inverse_ref[g, rows, :] = inverse[g * TILE : (g + 1) * TILE]
            attended_ref[rows, g * HEAD_SIZE : (g + 1) * HEAD_SIZE] = attended[
                g * TILE : (g + 1) * TILE
            ]
        return 0

    lax.fori_loop(0, tokens // TILE, tile, 0)
    term = dot(attended_ref[...], readout_ref[...], (1, 0))

    @pl.when(pl.program_id(0) == 0)
    def _():
        total[...] = term

    @pl.when(pl.program_id(0) == 1)
    def _():
        terms_ref[...] = (total[...] + term).astype(jnp.bfloat16)


def backward_kernel(
    dlogits_ref, readout_ref, q_ref, raised_ref, inverse_ref, attended_ref, second, first, own,
    q_grad_ref, to_second, to_first, to_own,
    keys, values, query, upstream, key_sum, value_sum,
):
    tokens, reach = q_ref.shape[0], WINDOW_KEYS + TILE
    fill_window(second, first, own, keys, values)
    for g in range(2):
        unit, _ = unit_of(q_ref[:, g * HEAD_SIZE : (g + 1) * HEAD_SIZE])
        query[g] = unit.astype(jnp.bfloat16)
    upstream[...] = dot(dlogits_ref[...], readout_ref[...], (1, 1))
    key_sum[...] = jnp.zeros_like(key_sum)
    value_sum[...] = jnp.zeros_like(value_sum)

    def tile(t, _):
        at = pl.multiple_of(t * TILE, TILE)
        window = pl.ds(at, reach)
        rows = pl.ds(at, TILE)
        scaled, offset = [], []
        for g in range(2):
            columns = slice(g * HEAD_SIZE, (g + 1) * HEAD_SIZE)
            grad = upstream[rows, columns] * inverse_ref[g, rows, :]
            offset.append(
                jnp.sum(grad * attended_ref[rows, columns].astype(jnp.float32), axis=-1, keepdims=True)
            )
            scaled.append(grad.astype(jnp.bfloat16))
        scaled = jnp.concatenate(scaled, axis=0)
        offset = jnp.concatenate(offset, axis=0)
        raised = jnp.concatenate([raised_ref[0, rows, :], raised_ref[1, rows, :]], axis=0)
        both = jnp.concatenate([query[0, rows, :], query[1, rows, :]], axis=0)
        weights = dot(scaled, values[window, :], (1, 1))
        scores = (raised.astype(jnp.float32) * (weights - offset)).astype(jnp.bfloat16)
        value_sum[window, :] += dot(raised, scaled, (0, 0))
        key_sum[window, :] += dot(scores, both, (0, 0))
        hat = dot(scores, keys[window, :], (1, 0)) * score_scale
        for g in range(2):
            columns = slice(g * HEAD_SIZE, (g + 1) * HEAD_SIZE)
            unit, inverse = unit_of(q_ref[rows, columns])
            part = hat[g * TILE : (g + 1) * TILE]
            q_grad_ref[rows, columns] = inverse * (
                part - unit * jnp.mean(unit * part, axis=-1, keepdims=True)
            )
        return 0

    lax.fori_loop(0, tokens // TILE, tile, 0)
    for n, out in enumerate((to_second, to_first, to_own)):
        part = slice(n * tokens, (n + 1) * tokens)
        out[0] = (key_sum[part, :] * score_scale).astype(out.dtype)
        out[1] = value_sum[part, :].astype(out.dtype)


def normalize_kernel(projected_ref, out):
    width = out.shape[2]
    for low in range(0, width, HEAD_SIZE):
        columns = slice(low, low + HEAD_SIZE)
        out[0, :, columns] = unit_of(projected_ref[:, columns])[0].astype(jnp.bfloat16)
    out[1] = projected_ref[:, width:].astype(jnp.bfloat16)


def normalized(projected):
    tokens, width = projected.shape
    return pl.pallas_call(
        normalize_kernel,
        out_shape=jax.ShapeDtypeStruct((2, tokens, width // 2), jnp.bfloat16),
        cost_estimate=pl.CostEstimate(
            flops=2_000_000, bytes_accessed=1_500_000, transcendentals=1024
        ),
        compiler_params=pltpu.CompilerParams(vmem_limit_bytes=SMALL_VMEM),
        name="normalized",
    )(projected)


def gradients_kernel(seq_ref, projected_ref, own, crossed, arrived, out):
    width = own.shape[2]
    keep = 1.0 - (seq_ref[0] % CORES).astype(jnp.float32)
    for low in range(0, width, HEAD_SIZE):
        columns = slice(low, low + HEAD_SIZE)
        unit, inverse = unit_of(projected_ref[:, columns])
        keys, values = (
            own[n, :, columns]
            + arrived[n, :, columns].astype(jnp.float32)
            + keep * crossed[n, :, columns].astype(jnp.float32)
            for n in range(2)
        )
        keys = inverse * (keys - unit * jnp.mean(unit * keys, axis=-1, keepdims=True))
        out[:, columns] = keys.astype(jnp.bfloat16)
        out[:, width + low : width + low + HEAD_SIZE] = values.astype(jnp.bfloat16)


def projection_gradients(seq, projected, own, crossed, arrived):
    vmem = pl.BlockSpec(memory_space=pltpu.VMEM)
    return pl.pallas_call(
        gradients_kernel,
        in_specs=[pl.BlockSpec(memory_space=pltpu.SMEM), vmem, vmem, vmem, vmem],
        out_specs=vmem,
        out_shape=jax.ShapeDtypeStruct(projected.shape, jnp.bfloat16),
        cost_estimate=pl.CostEstimate(
            flops=4_000_000, bytes_accessed=3_500_000, transcendentals=1024
        ),
        compiler_params=pltpu.CompilerParams(vmem_limit_bytes=SMALL_VMEM),
        name="projection_gradients",
    )(seq.reshape(1), projected, own, crossed, arrived)


def window_specs(tokens):
    return [pl.BlockSpec((2, tokens, HEAD_SIZE), lambda k: (0, 0, k))] * 3


def attention_forward(seq, queries, second, first, own, readout):
    tokens, width = queries.shape
    kv_heads, reach = own.shape[2] // HEAD_SIZE, WINDOW_KEYS + TILE
    candidates = readout.shape[1]
    return pl.pallas_call(
        forward_kernel,
        grid=(kv_heads,),
        in_specs=[
            pl.BlockSpec(memory_space=pltpu.SMEM),
            pl.BlockSpec((tokens, 2 * HEAD_SIZE), lambda k: (0, k)),
            *window_specs(tokens),
            pl.BlockSpec((2 * HEAD_SIZE, candidates), lambda k: (k, 0)),
        ],
        out_specs=[
            pl.BlockSpec((2, tokens, reach), lambda k: (k, 0, 0)),
            pl.BlockSpec((2, tokens, 1), lambda k: (k, 0, 0)),
            pl.BlockSpec((tokens, 2 * HEAD_SIZE), lambda k: (0, k)),
            pl.BlockSpec((tokens, candidates), lambda k: (0, 0)),
        ],
        out_shape=[
            jax.ShapeDtypeStruct((2 * kv_heads, tokens, reach), jnp.bfloat16),
            jax.ShapeDtypeStruct((2 * kv_heads, tokens, 1), jnp.float32),
            jax.ShapeDtypeStruct((tokens, width), jnp.bfloat16),
            jax.ShapeDtypeStruct((tokens, candidates), jnp.bfloat16),
        ],
        scratch_shapes=[
            pltpu.VMEM((3 * tokens, HEAD_SIZE), jnp.bfloat16),
            pltpu.VMEM((3 * tokens, HEAD_SIZE), jnp.bfloat16),
            pltpu.VMEM((2, tokens, HEAD_SIZE), jnp.bfloat16),
            pltpu.VMEM((tokens, candidates), jnp.float32),
        ],
        compiler_params=pltpu.CompilerParams(
            dimension_semantics=("arbitrary",), vmem_limit_bytes=ATTENTION_VMEM
        ),
        cost_estimate=pl.CostEstimate(
            flops=2_500_000_000, bytes_accessed=8_000_000, transcendentals=2_400_000
        ),
        name="attention_forward",
    )(seq.reshape(1), queries, second, first, own, readout)


def attention_backward(dlogits, readout, queries, raised, inverse, attended, second, first, own):
    tokens, width = queries.shape
    kv_heads, reach = own.shape[2] // HEAD_SIZE, WINDOW_KEYS + TILE
    candidates = readout.shape[1]
    pair = pl.BlockSpec((tokens, 2 * HEAD_SIZE), lambda k: (0, k))
    return pl.pallas_call(
        backward_kernel,
        grid=(kv_heads,),
        in_specs=[
            pl.BlockSpec((tokens, candidates), lambda k: (0, 0)),
            pl.BlockSpec((2 * HEAD_SIZE, candidates), lambda k: (k, 0)),
            pair,
            pl.BlockSpec((2, tokens, reach), lambda k: (k, 0, 0)),
            pl.BlockSpec((2, tokens, 1), lambda k: (k, 0, 0)),
            pair,
            *window_specs(tokens),
        ],
        out_specs=[pair, *window_specs(tokens)],
        out_shape=[
            jax.ShapeDtypeStruct((tokens, width), jnp.float32),
            jax.ShapeDtypeStruct(own.shape, jnp.bfloat16),
            jax.ShapeDtypeStruct(own.shape, jnp.bfloat16),
            jax.ShapeDtypeStruct(own.shape, jnp.float32),
        ],
        scratch_shapes=[
            pltpu.VMEM((3 * tokens, HEAD_SIZE), jnp.bfloat16),
            pltpu.VMEM((3 * tokens, HEAD_SIZE), jnp.bfloat16),
            pltpu.VMEM((2, tokens, HEAD_SIZE), jnp.bfloat16),
            pltpu.VMEM((tokens, 2 * HEAD_SIZE), jnp.float32),
            pltpu.VMEM((3 * tokens, HEAD_SIZE), jnp.float32),
            pltpu.VMEM((3 * tokens, HEAD_SIZE), jnp.float32),
        ],
        compiler_params=pltpu.CompilerParams(
            dimension_semantics=("arbitrary",), vmem_limit_bytes=ATTENTION_VMEM
        ),
        cost_estimate=pl.CostEstimate(
            flops=5_000_000_000, bytes_accessed=12_000_000, transcendentals=0
        ),
        name="attention_backward",
    )(dlogits, readout, queries, raised, inverse, attended, second, first, own)


def shards(inputs, queries, key_matrix, value_matrix, readout, token_mask, targets):
    tokens = inputs.shape[0]
    heads = lax.axis_size("head")
    seq = lax.axis_index("seq")
    core = seq % CORES
    own_weight = jnp.concatenate([key_matrix, value_matrix], axis=1)
    moved = moved_to_head(own_weight)
    full_weight = gathered_weights(own_weight)
    projected = jnp.dot(inputs, full_weight, preferred_element_type=jnp.float32)
    paired = normalized(projected)
    second = along(paired, 2)
    first = lax.ppermute(jnp.where(core == 0, paired, second), "seq", CORE_SWAP)
    rows_weight = gathered_rows(after(moved, second))
    raised, inverse, attended, partial_value = attention_forward(
        seq, queries, second, first, paired, readout
    )


    share = tokens // heads
    terms = lax.all_to_all(partial_value, "head", 0, 0, tiled=True)
    logits = jnp.sum(terms.astype(jnp.float32).reshape(heads, share, -1), axis=0)
    mine = lax.axis_index("head") * share
    wanted = lax.dynamic_slice_in_dim(targets, mine, share, 0)
    chosen = lax.dynamic_slice_in_dim(token_mask, mine, share, 0).astype(jnp.float32)[:, None]
    capped = softcap * jnp.tanh(logits / softcap)
    expo = jnp.exp(capped)
    probs = expo / jnp.sum(expo, axis=-1, keepdims=True)
    onehot = (wanted[:, None] == jnp.arange(logits.shape[1], dtype=jnp.int32)[None, :]).astype(
        jnp.float32
    )
    dlogits = (chosen * (probs - onehot) * (1.0 - (capped / softcap) ** 2)).astype(jnp.bfloat16)
    dlogits = lax.all_to_all(
        jnp.broadcast_to(dlogits[None], (heads,) + dlogits.shape), "head", 0, 0, tiled=True
    ).reshape(tokens, -1)

    query_grad, to_second, to_first, total = attention_backward(
        dlogits, readout, queries, raised, inverse, attended, second, first, paired
    )
    crossed = lax.ppermute(to_first, "seq", CORE_SWAP)
    outgoing = to_second.astype(jnp.float32) + jnp.where(core == 1, crossed, 0).astype(jnp.float32)
    arrived = along(outgoing.astype(jnp.bfloat16), -2)
    both_grad = projection_gradients(seq, projected, total, crossed, arrived)
    input_grad = head_product(rows_weight, both_grad).T
    return (query_grad, input_grad)


def solution(mesh):
    in_specs = (
        P("seq", None),
        P("seq", "head"),
        P("seq", "head"),
        P("seq", "head"),
        P("head", None),
        P("seq"),
        P("seq"),
    )
    out_specs = (P("seq", "head"), P("seq", "head"))
    return jax.shard_map(shards, mesh=mesh, in_specs=in_specs, out_specs=out_specs, check_vma=False)
```

```python
import jax
import jax.numpy as jnp
from jax import lax
from jax.experimental import pallas as pl
from jax.experimental.pallas import tpu as pltpu
from jax.sharding import PartitionSpec as P

HEAD_SIZE = 128
WINDOW_KEYS = 1024

norm_eps = 1e-06
softcap = 30.0
score_scale = 168.0 ** (-0.5)
LOG2_E = 1.4426950408889634

Y_LO, Z, CORES = 2, 8, 2
Y_HI, X = 2, 4


def seq_pairs(move):
    pairs = []
    for y in range(Y_LO):
        for z in range(Z):
            for c in range(CORES):
                ty, tz, tc = move(y, z, c)
                pairs.append(((y * Z + z) * CORES + c, (ty * Z + tz) * CORES + tc))
    return pairs


CORE_SWAP = seq_pairs(lambda y, z, c: (y, z, 1 - c))
Y_SWAP = seq_pairs(lambda y, z, c: (1 - y, z, c))
Z_UP = seq_pairs(lambda y, z, c: (y, (z + 1) % Z, c))
Z_DOWN = seq_pairs(lambda y, z, c: (y, (z - 1) % Z, c))


def head_pairs(flip, steps):
    return [
        (y * X + x, (y ^ flip) * X + (x + steps) % X) for y in range(Y_HI) for x in range(X)
    ]


X_UP, X_DOWN, Y_HI_SWAP = head_pairs(0, 1), head_pairs(0, -1), head_pairs(1, 0)


def after(value, other):
    corner = other[(slice(0, 1),) * other.ndim].reshape((1,) * value.ndim)
    return value + (corner * 0).astype(value.dtype)


def moved_to_head(own):
    heads = Y_HI * X
    pairs = []
    for y in range(Y_HI):
        for x in range(X):
            for p in range(Y_HI):
                for q in range(X):
                    for low in range(2):
                        for core in range(CORES):
                            source = (y * Z + 2 * x + low) * CORES + core
                            target = (p * Z + (2 * (x + q) + low) % Z) * CORES + core
                            pairs.append((source * heads + p * X + q, target * heads + y * X + x))
    return lax.ppermute(own, ("seq", "head"), pairs)


def gathered_rows(moved):
    columns = moved.shape[1]
    return lax.all_gather(moved, "seq", axis=0, tiled=True).reshape(Y_HI * X, -1, columns)


def head_product(weight, own):
    head = lax.axis_index("head")
    y, x = head // X, head % X

    def send(value, pairs):
        return lax.ppermute(value, "head", pairs)

    def term(value, flip, steps):
        block = lax.dynamic_index_in_dim(
            weight, (y ^ flip) * X + jnp.mod(2 * x - steps, X), 0, keepdims=False
        )
        return lax.dot_general(
            block, value, (((1,), (1,)), ((), ())), preferred_element_type=jnp.float32
        )

    half = own.shape[0] // 2
    below, above, across = send(own, X_UP), send(own, X_DOWN), send(own, Y_HI_SWAP)
    halves = (send(below[:half], X_UP), send(above[half:], X_DOWN))
    far = jnp.concatenate(halves)
    across_below, across_above = send(across, X_UP), send(across, X_DOWN)
    across_far = jnp.concatenate([send(part, Y_HI_SWAP) for part in halves])
    total = term(own, 0, 0)
    for value, flip, steps in (
        (below, 0, 1),
        (above, 0, -1),
        (across, 1, 0),
        (far, 0, 2),
        (across_below, 1, 1),
        (across_above, 1, -1),
    ):
        total = total + term(value, flip, steps)
    return lax.optimization_barrier(total) + term(across_far, 1, 2)


def along(value, steps):
    count = lax.axis_size("seq")
    first, last = max(0, -steps), min(count, count - steps)
    return lax.ppermute(value, "seq", [(i, i + steps) for i in range(first, last)])


def gathered_weights(own):
    rows, columns = own.shape
    seq = lax.axis_index("seq")
    y, z, core = seq // (Z * CORES), (seq // CORES) % Z, seq % CORES
    other = lax.ppermute(own, "seq", Y_SWAP)
    low = jnp.where(y == 0, own, other)
    high = jnp.where(y == 0, other, own)
    pair = jnp.stack([low, high])
    full = jnp.zeros((Y_LO, Z, CORES, rows, columns), own.dtype)

    def put(full, blocks):
        offsets = list(blocks)
        swapped = lax.ppermute(jnp.concatenate(list(blocks.values())), "seq", CORE_SWAP)
        for n, offset in enumerate(offsets):
            at = jnp.mod(z + offset, Z)
            for piece, c in ((blocks[offset], core), (swapped[2 * n : 2 * n + 2], 1 - core)):
                full = lax.dynamic_update_slice(full, piece[:, None, None], (0, at, c, 0, 0))
        return full

    up = down = pair
    full = put(full, {0: pair})
    for k in range(1, Z // 2):
        up = lax.ppermute(up, "seq", Z_UP)
        down = lax.ppermute(down, "seq", Z_DOWN)
        full = put(full, {-k: up, k: down})
    last = jnp.stack(
        [lax.ppermute(up[0], "seq", Z_UP), lax.ppermute(down[1], "seq", Z_DOWN)]
    )
    full = put(full, {Z // 2: last})
    return full.reshape(Y_LO * Z * CORES * rows, columns)


TILE = 128
FORWARD_VMEM, BACKWARD_VMEM = 50 << 20, 50 << 20
SMALL_VMEM = 16 << 20


def dot(a, b, contract):
    return lax.dot_general(a, b, ((contract[:1], contract[1:]), ((), ())), preferred_element_type=jnp.float32)


def unit_of(rows):
    rows = rows.astype(jnp.float32)
    inverse = lax.rsqrt(jnp.mean(rows * rows, axis=-1, keepdims=True) + norm_eps)
    return rows * inverse, inverse


def fill_window(second, first, own, keys, values):
    tokens = own.shape[1]
    for n, part in enumerate((second, first, own)):
        keys[n * tokens : (n + 1) * tokens, :] = part[0]
        values[n * tokens : (n + 1) * tokens, :] = part[1]


def forward_kernel(
    seq_ref, q_ref, second, first, own, readout_ref,
    raised_ref, inverse_ref, attended_ref, terms_ref, keys, values, query, total,
):
    tokens, reach = q_ref.shape[0], WINDOW_KEYS + TILE
    fill_window(second, first, own, keys, values)
    for g in range(2):
        unit, _ = unit_of(q_ref[:, g * HEAD_SIZE : (g + 1) * HEAD_SIZE])
        query[g] = (unit * (score_scale * LOG2_E)).astype(jnp.bfloat16)
    oldest = tokens * jnp.maximum(2 - seq_ref[0], 0)
    row = lax.broadcasted_iota(jnp.int32, (2 * TILE, TILE), 0) % TILE
    column = lax.broadcasted_iota(jnp.int32, (2 * TILE, TILE), 1)
    newer = (column > row).astype(jnp.float32)
    older = (column <= row).astype(jnp.float32)

    def tile(t, _):
        at = pl.multiple_of(t * TILE, TILE)
        window = pl.ds(at, reach)
        rows = pl.ds(at, TILE)
        both = jnp.concatenate([query[0, rows, :], query[1, rows, :]], axis=0)
        place = at + lax.broadcasted_iota(jnp.int32, (1, reach), 1)
        seen = (place >= oldest).astype(jnp.float32)
        raised = jnp.exp2(dot(both, keys[window, :], (1, 1))) * seen
        raised = jnp.concatenate(
            [raised[:, :TILE] * newer, raised[:, TILE:-TILE], raised[:, -TILE:] * older], axis=1
        )
        inverse = 1.0 / jnp.sum(raised, axis=-1, keepdims=True)
        kept = raised.astype(jnp.bfloat16)
        attended = (dot(kept, values[window, :], (1, 0)) * inverse).astype(jnp.bfloat16)
        for g in range(2):
            raised_ref[g, rows, :] = kept[g * TILE : (g + 1) * TILE]
            inverse_ref[g, rows, :] = inverse[g * TILE : (g + 1) * TILE]
            attended_ref[rows, g * HEAD_SIZE : (g + 1) * HEAD_SIZE] = attended[
                g * TILE : (g + 1) * TILE
            ]
        return 0

    lax.fori_loop(0, tokens // TILE, tile, 0)
    term = dot(attended_ref[...], readout_ref[...], (1, 0))

    @pl.when(pl.program_id(0) == 0)
    def _():
        total[...] = term

    @pl.when(pl.program_id(0) == 1)
    def _():
        terms_ref[...] = (total[...] + term).astype(jnp.bfloat16)


def backward_kernel(
    dlogits_ref, readout_ref, q_ref, raised_ref, inverse_ref, attended_ref, second, first, own,
    q_grad_ref, to_second, to_first, to_own,
    keys, values, query, upstream, key_sum, value_sum,
):
    tokens, reach = q_ref.shape[0], WINDOW_KEYS + TILE
    fill_window(second, first, own, keys, values)
    for g in range(2):
        unit, _ = unit_of(q_ref[:, g * HEAD_SIZE : (g + 1) * HEAD_SIZE])
        query[g] = unit.astype(jnp.bfloat16)
    upstream[...] = dot(dlogits_ref[...], readout_ref[...], (1, 1))
    key_sum[...] = jnp.zeros_like(key_sum)
    value_sum[...] = jnp.zeros_like(value_sum)

    def tile(t, _):
        at = pl.multiple_of(t * TILE, TILE)
        window = pl.ds(at, reach)
        rows = pl.ds(at, TILE)
        scaled, offset = [], []
        for g in range(2):
            columns = slice(g * HEAD_SIZE, (g + 1) * HEAD_SIZE)
            grad = upstream[rows, columns] * inverse_ref[g, rows, :]
            offset.append(
                jnp.sum(grad * attended_ref[rows, columns].astype(jnp.float32), axis=-1, keepdims=True)
            )
            scaled.append(grad.astype(jnp.bfloat16))
        scaled = jnp.concatenate(scaled, axis=0)
        offset = jnp.concatenate(offset, axis=0)
        raised = jnp.concatenate([raised_ref[0, rows, :], raised_ref[1, rows, :]], axis=0)
        both = jnp.concatenate([query[0, rows, :], query[1, rows, :]], axis=0)
        weights = dot(scaled, values[window, :], (1, 1))
        scores = (raised.astype(jnp.float32) * (weights - offset)).astype(jnp.bfloat16)
        value_sum[window, :] += dot(raised, scaled, (0, 0))
        key_sum[window, :] += dot(scores, both, (0, 0))
        hat = dot(scores, keys[window, :], (1, 0)) * score_scale
        for g in range(2):
            columns = slice(g * HEAD_SIZE, (g + 1) * HEAD_SIZE)
            unit, inverse = unit_of(q_ref[rows, columns])
            part = hat[g * TILE : (g + 1) * TILE]
            q_grad_ref[rows, columns] = inverse * (
                part - unit * jnp.mean(unit * part, axis=-1, keepdims=True)
            )
        return 0

    lax.fori_loop(0, tokens // TILE, tile, 0)
    for n, out in enumerate((to_second, to_first, to_own)):
        part = slice(n * tokens, (n + 1) * tokens)
        out[0] = (key_sum[part, :] * score_scale).astype(out.dtype)
        out[1] = value_sum[part, :].astype(out.dtype)


def normalize_kernel(projected_ref, out):
    width = out.shape[2]
    for low in range(0, width, HEAD_SIZE):
        columns = slice(low, low + HEAD_SIZE)
        out[0, :, columns] = unit_of(projected_ref[:, columns])[0].astype(jnp.bfloat16)
    out[1] = projected_ref[:, width:].astype(jnp.bfloat16)


def normalized(projected):
    tokens, width = projected.shape
    return pl.pallas_call(
        normalize_kernel,
        out_shape=jax.ShapeDtypeStruct((2, tokens, width // 2), jnp.bfloat16),
        cost_estimate=pl.CostEstimate(
            flops=2_000_000, bytes_accessed=1_500_000, transcendentals=1024
        ),
        compiler_params=pltpu.CompilerParams(vmem_limit_bytes=SMALL_VMEM),
        name="normalized",
    )(projected)


def gradients_kernel(projected_ref, own, arrived, out):
    width = own.shape[2]
    for low in range(0, width, HEAD_SIZE):
        columns = slice(low, low + HEAD_SIZE)
        unit, inverse = unit_of(projected_ref[:, columns])
        keys, values = (
            own[n, :, columns] + arrived[n, :, columns].astype(jnp.float32) for n in range(2)
        )
        keys = inverse * (keys - unit * jnp.mean(unit * keys, axis=-1, keepdims=True))
        out[:, columns] = keys.astype(jnp.bfloat16)
        out[:, width + low : width + low + HEAD_SIZE] = values.astype(jnp.bfloat16)


def projection_gradients(projected, own, arrived):
    vmem = pl.BlockSpec(memory_space=pltpu.VMEM)
    return pl.pallas_call(
        gradients_kernel,
        in_specs=[vmem] * 3,
        out_specs=vmem,
        out_shape=jax.ShapeDtypeStruct(projected.shape, jnp.bfloat16),
        cost_estimate=pl.CostEstimate(
            flops=4_000_000, bytes_accessed=3_500_000, transcendentals=1024
        ),
        compiler_params=pltpu.CompilerParams(vmem_limit_bytes=SMALL_VMEM),
        name="projection_gradients",
    )(projected, own, arrived)


def window_specs(tokens):
    return [pl.BlockSpec((2, tokens, HEAD_SIZE), lambda k: (0, 0, k))] * 3


def attention_forward(seq, queries, second, first, own, readout):
    tokens, width = queries.shape
    kv_heads, reach = own.shape[2] // HEAD_SIZE, WINDOW_KEYS + TILE
    candidates = readout.shape[1]
    return pl.pallas_call(
        forward_kernel,
        grid=(kv_heads,),
        in_specs=[
            pl.BlockSpec(memory_space=pltpu.SMEM),
            pl.BlockSpec((tokens, 2 * HEAD_SIZE), lambda k: (0, k)),
            *window_specs(tokens),
            pl.BlockSpec((2 * HEAD_SIZE, candidates), lambda k: (k, 0)),
        ],
        out_specs=[
            pl.BlockSpec((2, tokens, reach), lambda k: (k, 0, 0)),
            pl.BlockSpec((2, tokens, 1), lambda k: (k, 0, 0)),
            pl.BlockSpec((tokens, 2 * HEAD_SIZE), lambda k: (0, k)),
            pl.BlockSpec((tokens, candidates), lambda k: (0, 0)),
        ],
        out_shape=[
            jax.ShapeDtypeStruct((2 * kv_heads, tokens, reach), jnp.bfloat16),
            jax.ShapeDtypeStruct((2 * kv_heads, tokens, 1), jnp.float32),
            jax.ShapeDtypeStruct((tokens, width), jnp.bfloat16),
            jax.ShapeDtypeStruct((tokens, candidates), jnp.bfloat16),
        ],
        scratch_shapes=[
            pltpu.VMEM((3 * tokens, HEAD_SIZE), jnp.bfloat16),
            pltpu.VMEM((3 * tokens, HEAD_SIZE), jnp.bfloat16),
            pltpu.VMEM((2, tokens, HEAD_SIZE), jnp.bfloat16),
            pltpu.VMEM((tokens, candidates), jnp.float32),
        ],
        compiler_params=pltpu.CompilerParams(
            dimension_semantics=("arbitrary",), vmem_limit_bytes=FORWARD_VMEM
        ),
        cost_estimate=pl.CostEstimate(
            flops=2_500_000_000, bytes_accessed=8_000_000, transcendentals=2_400_000
        ),
        name="attention_forward",
    )(seq.reshape(1), queries, second, first, own, readout)


def attention_backward(dlogits, readout, queries, raised, inverse, attended, second, first, own):
    tokens, width = queries.shape
    kv_heads, reach = own.shape[2] // HEAD_SIZE, WINDOW_KEYS + TILE
    candidates = readout.shape[1]
    pair = pl.BlockSpec((tokens, 2 * HEAD_SIZE), lambda k: (0, k))
    return pl.pallas_call(
        backward_kernel,
        grid=(kv_heads,),
        in_specs=[
            pl.BlockSpec((tokens, candidates), lambda k: (0, 0)),
            pl.BlockSpec((2 * HEAD_SIZE, candidates), lambda k: (k, 0)),
            pair,
            pl.BlockSpec((2, tokens, reach), lambda k: (k, 0, 0)),
            pl.BlockSpec((2, tokens, 1), lambda k: (k, 0, 0)),
            pair,
            *window_specs(tokens),
        ],
        out_specs=[pair, *window_specs(tokens)],
        out_shape=[
            jax.ShapeDtypeStruct((tokens, width), jnp.float32),
            jax.ShapeDtypeStruct(own.shape, jnp.bfloat16),
            jax.ShapeDtypeStruct(own.shape, jnp.bfloat16),
            jax.ShapeDtypeStruct(own.shape, jnp.float32),
        ],
        scratch_shapes=[
            pltpu.VMEM((3 * tokens, HEAD_SIZE), jnp.bfloat16),
            pltpu.VMEM((3 * tokens, HEAD_SIZE), jnp.bfloat16),
            pltpu.VMEM((2, tokens, HEAD_SIZE), jnp.bfloat16),
            pltpu.VMEM((tokens, 2 * HEAD_SIZE), jnp.float32),
            pltpu.VMEM((3 * tokens, HEAD_SIZE), jnp.float32),
            pltpu.VMEM((3 * tokens, HEAD_SIZE), jnp.float32),
        ],
        compiler_params=pltpu.CompilerParams(
            dimension_semantics=("arbitrary",), vmem_limit_bytes=BACKWARD_VMEM
        ),
        cost_estimate=pl.CostEstimate(
            flops=5_000_000_000, bytes_accessed=12_000_000, transcendentals=0
        ),
        name="attention_backward",
    )(dlogits, readout, queries, raised, inverse, attended, second, first, own)


def shards(inputs, queries, key_matrix, value_matrix, readout, token_mask, targets):
    tokens = inputs.shape[0]
    heads = lax.axis_size("head")
    seq = lax.axis_index("seq")
    core = seq % CORES
    own_weight = jnp.concatenate([key_matrix, value_matrix], axis=1)
    moved = moved_to_head(own_weight)
    full_weight = gathered_weights(own_weight)
    projected = jnp.dot(inputs, full_weight, preferred_element_type=jnp.float32)
    paired = normalized(projected)
    second = along(paired, 2)
    first = lax.ppermute(jnp.where(core == 0, paired, second), "seq", CORE_SWAP)
    rows_weight = gathered_rows(after(moved, second))
    raised, inverse, attended, partial_value = attention_forward(
        seq, queries, second, first, paired, readout
    )


    share = tokens // heads
    terms = lax.all_to_all(partial_value, "head", 0, 0, tiled=True)
    logits = jnp.sum(terms.astype(jnp.float32).reshape(heads, share, -1), axis=0)
    mine = lax.axis_index("head") * share
    wanted = lax.dynamic_slice_in_dim(targets, mine, share, 0)
    chosen = lax.dynamic_slice_in_dim(token_mask, mine, share, 0).astype(jnp.float32)[:, None]
    capped = softcap * jnp.tanh(logits / softcap)
    expo = jnp.exp(capped)
    probs = expo / jnp.sum(expo, axis=-1, keepdims=True)
    onehot = (wanted[:, None] == jnp.arange(logits.shape[1], dtype=jnp.int32)[None, :]).astype(
        jnp.float32
    )
    dlogits = (chosen * (probs - onehot) * (1.0 - (capped / softcap) ** 2)).astype(jnp.bfloat16)
    dlogits = lax.all_to_all(
        jnp.broadcast_to(dlogits[None], (heads,) + dlogits.shape), "head", 0, 0, tiled=True
    ).reshape(tokens, -1)

    query_grad, to_second, to_first, total = attention_backward(
        dlogits, readout, queries, raised, inverse, attended, second, first, paired
    )
    crossed = lax.ppermute(to_first, "seq", CORE_SWAP)
    outgoing = to_second.astype(jnp.float32) + jnp.where(core == 1, crossed, 0).astype(jnp.float32)
    arrived = along(outgoing.astype(jnp.bfloat16), -2)
    total = total + jnp.where(core == 0, crossed, 0).astype(jnp.float32)
    both_grad = projection_gradients(projected, total, arrived)
    input_grad = head_product(rows_weight, both_grad).T
    return (query_grad, input_grad)


def solution(mesh):
    in_specs = (
        P("seq", None),
        P("seq", "head"),
        P("seq", "head"),
        P("seq", "head"),
        P("head", None),
        P("seq"),
        P("seq"),
    )
    out_specs = (P("seq", "head"), P("seq", "head"))
    return jax.shard_map(shards, mesh=mesh, in_specs=in_specs, out_specs=out_specs, check_vma=False)
```
